32 devices in a mesh: freq: 2 (over x), grp: 4 (over z), sub: 4 (over y, core).
Axes of the slice: x: 2, y: 2, z: 4, core: 2. Of those that a mesh axis runs over, the one named last changes fastest.
Arguments:
- alm: bfloat16 [256, 16, 2, 1024], P('freq', ('grp', 'sub')), may hold values from -6 to 6
- band_index: int32 [32, 32], replicated, may hold values from 0 to 255
- band_weight: float32 [32, 32], replicated, may hold values from 0.05 to 0.5
- legendre: bfloat16 [16, 1024, 1024], P(('grp', 'sub')), may hold values from -0.03125 to 0.03125
- orders: int32 [16], replicated, may hold values from 0 to 1023, as said below
- owner: int32 [32768, 1], P(('grp', 'sub')), may hold values from 0 to 15; in each aligned block of 2048 rows (0 to 2047, 2048 to 4095, ...) at most 192 rows name the same one
- tile_local: int32 [32768], P(('grp', 'sub')), may hold values from 0 to 127
- interp: bfloat16 [32768, 512], P(('grp', 'sub')), may hold values from -0.25 to 0.25
Outputs:
- tod: bfloat16 [32768, 32], P(('grp', 'sub'), 'freq')
The draws below stay inside these ranges and needn't reach their ends.
Inputs may be any that keep to these rules, and one draw needn't show every extreme that they name: 16 distinct orders; 0 and 1023 are always among them. `owner`: among the 2048 samples of one index of grp and sub (aligned blocks of 2048 rows) no cycle band is named more than 192 times, a bound that some block reaches.
All inputs are finite; a program needn't handle non-finite values.
Results may differ from the reference program's by a relative error of at most 0.0073.
Values may be sent and summed in bfloat16 or wider, within the bound.
No kernel may reach another device: no remote copies, remote signals or barrier semaphores. Data moves between devices by JAX's collectives and lax.ppermute only.
A program may use at most 64 MiB of HBM per device.

```python
import math
import jax
import jax.numpy as jnp
import numpy as np
from jax import lax

FREQS = 256
DET = 32
K = 32
L = 1024
R = 1024
NPHI = 1024
TR = 4
TPHI = 128
SD = 2048
OWNERS = 16
M = 16
NT_DEV = 128
TPIX = 512
CAP = 192
S = 32768


def draw_orders(key, part):
    first_key, second_key = jax.random.split(jax.random.fold_in(key, 11))
    middle = jax.random.permutation(first_key, L - 2)[:M - 2] + 1
    values = jnp.concatenate([jnp.zeros((1,), jnp.int32), jnp.full((1,), L - 1, jnp.int32), middle.astype(jnp.int32)])
    return jax.random.permutation(second_key, values)


def plant(drawn, stream_key, smallest, largest):
    index_at = [jax.random.randint(jax.random.fold_in(stream_key, axis), (), 0, length) for axis, length in enumerate(drawn.shape)]
    longest = drawn.shape.index(max(drawn.shape))
    next_to = index_at[:longest] + [(index_at[longest] + 1) % drawn.shape[longest]] + index_at[longest + 1:]
    return drawn.at[tuple(index_at)].set(smallest).at[tuple(next_to)].set(largest)


def level_of(own_key, dims, cuts, least, largest):
    gain, own = 1.0, jax.random.fold_in(own_key, 6)
    for dim, blocks in cuts:
        heights = jnp.exp(jax.random.uniform(jax.random.fold_in(own, dim), (blocks,), jnp.float32, least / len(cuts), largest / len(cuts)))
        gain = gain * jnp.repeat(heights, dims[dim] // blocks).reshape([-1 if axis == dim else 1 for axis in range(len(dims))])
    return gain


def assign_block(rng, own, number, rows, count, top, limit, lean):
    ranking = jax.random.permutation(rng, count)
    heavy_load, usual = shares(count, rows * top, limit, lean, True), shares(count, rows * top, limit, lean, False)
    places = jnp.arange(count)

    def named(tallies, turn):
        used = int((tallies > 0).sum())
        fixed = max(1, used // 4)
        passed = fixed + (places - fixed + turn * (used - fixed)) % max(1, count - fixed)
        return jnp.zeros((count,), jnp.int32).at[ranking[jnp.where(places < fixed, places, passed)]].set(jnp.asarray(tallies, jnp.int32))

    tallies = jnp.where(number % 4 == 0, named(heavy_load, number // 4), named(usual, number - number // 4 - 1))
    mixed = jax.random.permutation(jax.random.fold_in(own, 3), count)
    donor, sink = mixed[0:count // 2 * 2:2], mixed[1:count // 2 * 2:2]
    margin = jnp.minimum(tallies[donor] - 1, limit - tallies[sink]) // 2
    margin = jnp.where((donor == ranking[0]) | (sink == ranking[0]) | (tallies[sink] == 0), 0, jnp.maximum(margin, 0))
    passed = jax.random.randint(jax.random.fold_in(own, 4), (count // 2,), 0, 1 << 20) % (margin + 1)
    tallies = tallies.at[donor].add(-passed).at[sink].add(passed)
    labels = jnp.searchsorted(jnp.cumsum(tallies), jnp.arange(rows * top), side="right").astype(jnp.int32)
    listing = labels.reshape(top, rows).T
    listing = listing[jax.random.permutation(jax.random.fold_in(own, 1), rows)]
    turn = jax.random.randint(jax.random.fold_in(own, 2), (rows, 1), 0, top)
    return jnp.take_along_axis(listing, (jnp.arange(top)[None, :] + turn) % top, axis=1)


def shares(amount, total, limit, skew, full):
    portions = [(1 << 20) // math.isqrt(standing ** skew) + 1 for standing in range(1, amount + 1)]
    largest = limit if full else min(limit, max(-(-total // amount), total * portions[0] // sum(portions)))
    least = 1 if total - largest >= amount - 1 else 0
    holding, rest = [largest] + [least] * (amount - 1), total - largest - least * (amount - 1)
    while rest > 0:
        free = [i for i in range(1, amount) if holding[i] < largest] or [i for i in range(1, amount) if holding[i] < limit]
        whole, budget = sum([portions[i] for i in free]), rest
        for i in free:
            more = min(limit - holding[i], max(1, budget * portions[i] // whole), rest)
            holding[i] = holding[i] + more
            rest = rest - more
    return np.array(holding)


def gaussian(own_key, extent, scale, bound, cuts=(), held_as=jnp.bfloat16):
    array = scale * jax.random.normal(own_key, extent, jnp.float32)
    if cuts:
        array = array * level_of(own_key, extent, cuts, -0.22, 0.18)
    return jnp.clip(array, -bound, bound).astype(held_as)


def setup_inputs(seed: int = 0) -> dict:
    streams_of = jax.random.split(jax.random.key(seed), 9)
    alm = gaussian(streams_of[0], (FREQS, M, 2, L), 1.0, 6.0, ((0, 2), (1, 16)))
    band_index = plant(jax.random.randint(streams_of[1], (DET, K), 0, FREQS), jax.random.fold_in(streams_of[1], 1), 0, FREQS - 1).astype(jnp.int32)
    band_weight = jnp.clip(jnp.exp(jax.random.uniform(streams_of[2], (DET, K), jnp.float32, math.log(0.05), math.log(0.5))), 0.05, 0.5)
    legendre = gaussian(streams_of[3], (M, L, R), (2 * L * M) ** -0.5, 0.03125, ((0, 16),))
    orders = draw_orders(jax.random.fold_in(streams_of[8], 71), 0)
    owner_keys = jax.random.split(jax.random.fold_in(streams_of[5], 1), S // SD)
    owner_turns = jax.random.permutation(jax.random.fold_in(streams_of[5], 3), S // SD)
    owner = jax.vmap(lambda own, number: assign_block(jax.random.fold_in(streams_of[5], 2), own, number, SD, OWNERS, 1, CAP, 2))(owner_keys, owner_turns).reshape((S, 1))
    tile_local = plant(jax.random.randint(streams_of[6], (S,), 0, NT_DEV), jax.random.fold_in(streams_of[6], 1), 0, NT_DEV - 1).astype(jnp.int32)
    interp = gaussian(streams_of[7], (S, TPIX), TPIX ** -0.5, 0.25, ((0, 16),))
    return dict(alm=alm, band_index=band_index, band_weight=band_weight, legendre=legendre, orders=orders, owner=owner, tile_local=tile_local, interp=interp)


def band_matrix(band_index, band_weight, first_freq, freq_count):
    freq_ids = first_freq + lax.iota(jnp.int32, freq_count)
    matches = (band_index[:, :, None] == freq_ids[None, None, :]).astype(jnp.float32)
    return jnp.sum(matches * band_weight[:, :, None], axis=1).astype(jnp.bfloat16)


def phase_basis(order_list, longitudes):
    lon_index = lax.iota(jnp.int32, longitudes)
    phase_turns = (order_list[:, None] * lon_index[None, :]) % longitudes
    angles = phase_turns.astype(jnp.float32) * (2.0 * math.pi / longitudes)
    factor = jnp.where(order_list == 0, 1.0, 2.0).astype(jnp.float32)[:, None]
    return jnp.stack([factor * jnp.cos(angles), -factor * jnp.sin(angles)]).astype(jnp.bfloat16)


def reference(alm, band_index, band_weight, legendre, orders, owner, tile_local, interp):
    band_full = band_matrix(band_index, band_weight, 0, FREQS)
    flat_alm = alm.reshape(FREQS, M * 2 * L)
    detector_alm = jnp.dot(band_full, flat_alm, preferred_element_type=jnp.float32).astype(jnp.bfloat16)
    detector_alm = detector_alm.reshape(DET, M, 2, L)
    degree = lax.iota(jnp.int32, L)

    def one_order(member):
        coefs, table, order_value = member
        panel = jnp.where(degree[:, None] >= order_value, table, jnp.zeros_like(table))
        result = jnp.dot(coefs.reshape(DET * 2, L), panel, preferred_element_type=jnp.float32)
        return result.astype(jnp.bfloat16).reshape(DET, 2, R)

    cycle_coef = lax.map(one_order, (jnp.transpose(detector_alm, (1, 0, 2, 3)), legendre, orders))
    basis = phase_basis(orders, NPHI)
    sky = jnp.einsum("mdcr,cmj->drj", cycle_coef.astype(jnp.float32), basis.astype(jnp.float32))
    sky = sky.astype(jnp.bfloat16)
    cycle_tiles = R // TR
    lon_tiles = NPHI // TPHI
    tiles = sky.reshape(DET, cycle_tiles, TR, lon_tiles, TPHI).transpose(1, 3, 0, 2, 4)
    tiles = tiles.reshape(cycle_tiles * lon_tiles, DET, TR * TPHI)
    global_tile = owner[:, 0] * NT_DEV + tile_local
    block_rows = min(1024, S)
    if S % block_rows != 0:
        block_rows = S

    def one_block(member):
        weights, tile_ids = member
        picked = tiles[tile_ids].astype(jnp.float32)
        return jnp.einsum("bp,bdp->bd", weights.astype(jnp.float32), picked).astype(jnp.bfloat16)

    tod = lax.map(one_block, (interp.reshape(S // block_rows, block_rows, TR * TPHI), global_tile.reshape(S // block_rows, block_rows)))
    return tod.reshape(S, DET)
```

```python
import functools
import math

import jax
import jax.numpy as jnp
from jax import lax
from jax.experimental import pallas as pl
from jax.experimental.pallas import tpu as pltpu
from jax.sharding import PartitionSpec as P

NPHI = 1024
TR = 4
TPHI = 128
LANES = 128
F32 = jnp.float32
BF16 = jnp.bfloat16
CONTRACT_LAST = (((1,), (1,)), ((), ()))


def iota(shape, axis):
    return lax.broadcasted_iota(jnp.int32, shape, axis)


def band_kernel(index_ref, weight_ref, alm_ref, own_ref, send_ref):
    rows = alm_ref.shape[0]
    dets, entries = index_ref.shape
    half = dets // 2
    me = lax.axis_index("freq")
    column = iota((dets, rows), 1)
    wanted = me * (rows // 2) + lax.shift_right_logical(column, 1)
    band = jnp.zeros((dets, rows), F32)
    for k in range(entries):
        hit = index_ref[:, k : k + 1] == wanted
        band = band + jnp.where(hit, weight_ref[:, k : k + 1], 0.0)
    part = lax.bitwise_and(column[:half], 1)
    low, high = band[:half], band[half:]
    own = jnp.where(me == 0, low, high)
    other = jnp.where(me == 0, high, low)
    matrix = jnp.concatenate(
        [jnp.where(part == c, side, 0.0) for side in (own, other) for c in range(2)]
    ).astype(BF16)
    sums = jnp.dot(matrix, alm_ref[...], preferred_element_type=F32)
    own_ref[...] = sums[:dets]
    send_ref[...] = sums[dets:].astype(BF16)


def band_sums(band_index, band_weight, alm):
    rows, multipoles = alm.shape
    dets = band_index.shape[0]
    return pl.pallas_call(
        band_kernel,
        out_shape=(
            jax.ShapeDtypeStruct((dets, multipoles), F32),
            jax.ShapeDtypeStruct((dets, multipoles), BF16),
        ),
        name="band_sums",
    )(band_index, band_weight, alm)


def cycle_kernel(order_ref, own_ref, recv_ref, legendre_ref, out_ref):
    rows, multipoles = own_ref.shape
    half = rows // 2
    cycles = legendre_ref.shape[1]
    keep = iota((rows, multipoles), 1) >= order_ref[0]
    coefs = own_ref[...] + recv_ref[...].astype(F32)
    coefs = jnp.where(keep, coefs, 0.0).astype(BF16)
    table = jnp.dot(coefs, legendre_ref[...], preferred_element_type=F32)
    first = iota((half, LANES), 1) < LANES // 2
    for tile in range(cycles // LANES):
        both = table[:, tile * LANES : (tile + 1) * LANES]
        turned = pltpu.roll(both, LANES // 2, 1)
        even = jnp.where(first, both[:half], turned[half:])
        odd = jnp.where(first, turned[:half], both[half:])
        out_ref[pl.ds(2 * tile * half, half), :] = even.astype(BF16)
        out_ref[pl.ds((2 * tile + 1) * half, half), :] = odd.astype(BF16)


def cycle_coefs(order, own, received, legendre):
    rows, multipoles = own.shape
    cycles = legendre.shape[1]
    return pl.pallas_call(
        cycle_kernel,
        out_shape=jax.ShapeDtypeStruct((rows * cycles // LANES, LANES), BF16),
        in_specs=[pl.BlockSpec(memory_space=pltpu.SMEM)]
        + [pl.BlockSpec(memory_space=pltpu.VMEM)] * 3,
        name="cycle_coefs",
    )(order, own, received, legendre)


def spread_kernel(orders_ref, code_ref, interp_ref, x_ref, mark_ref, base_ref, fold_ref, copy_ref):
    rows = interp_ref.shape[0]
    parts = 2 * (LANES // (2 * TR))
    lon_tiles = NPHI // TPHI
    low_count = LANES // (2 * TR)
    wide = parts * low_count * TR
    span = lon_tiles * parts

    @pl.when(pl.program_id(0) == 0)
    def _():
        place = iota((TPHI, span), 0)
        lane = iota((TPHI, span), 1)
        longitude = place + TPHI * (lane // parts)
        order = jnp.broadcast_to(orders_ref[...], (TPHI, span))
        turns = order * longitude + (NPHI // 4) * (lane % 2)
        turns = lax.bitwise_and(turns, NPHI - 1)
        angle = turns.astype(F32) * (2.0 * math.pi / NPHI)
        factor = jnp.where(order == 0, 1.0, 2.0)
        base_ref[...] = (factor * jnp.cos(angle)).astype(BF16)
        row = iota((TR * span, LANES), 0)
        lane = iota((TR * span, LANES), 1)
        hit = (row // span == lane // parts) & (row % parts == lane % parts)
        fold_ref[...] = jnp.where(hit, 1.0, 0.0).astype(BF16)
        row = iota((LANES, wide), 0)
        lane = iota((LANES, wide), 1)
        hit = (row // parts == lane % TR) & (row % parts == lane // (low_count * TR))
        copy_ref[...] = jnp.where(hit, 1.0, 0.0).astype(BF16)

    groups = []
    for group in range(rows // LANES):
        line = code_ref[0, group : group + 1, :].astype(F32)
        groups.append(jnp.broadcast_to(line, (LANES, LANES)).T)
    code = jnp.concatenate(groups).astype(jnp.int32)
    lon_tile = lax.bitwise_and(code, lon_tiles - 1)
    cycle_tile = lax.shift_right_logical(code, lon_tiles.bit_length() - 1)
    low = lax.bitwise_and(cycle_tile, low_count - 1)
    mark_ref[...] = lax.shift_right_logical(cycle_tile, low_count.bit_length() - 1)

    lane = iota((rows, LANES), 1)
    masks = [
        lon_tile == (lane + LANES * block) // parts for block in range(span // LANES)
    ]
    pieces = []
    for i in range(TR):
        turned = jnp.dot(
            interp_ref[:, i * TPHI : (i + 1) * TPHI], base_ref[...], preferred_element_type=F32
        )
        for block, mask in enumerate(masks):
            piece = turned[:, block * LANES : (block + 1) * LANES]
            pieces.append(jnp.where(mask, piece, 0.0).astype(BF16))
    folded = jnp.dot(
        jnp.concatenate(pieces, axis=1), fold_ref[...], preferred_element_type=F32
    ).astype(BF16)
    mine = low == (lane // TR) % low_count
    for block in range(wide // LANES):
        cols = slice(block * LANES, (block + 1) * LANES)
        piece = jnp.dot(folded, copy_ref[:, cols], preferred_element_type=F32)
        x_ref[:, cols] = jnp.where(mine, piece, 0.0).astype(BF16)


def spread_samples(order_lanes, code, interp):
    samples, pixels = interp.shape
    rows = min(512, samples)
    parts = LANES // TR
    low_count = LANES // (2 * TR)
    wide = parts * low_count * TR
    span = (NPHI // TPHI) * parts
    steps = samples // rows
    return pl.pallas_call(
        spread_kernel,
        grid=(steps,),
        out_shape=(
            jax.ShapeDtypeStruct((samples, wide), BF16),
            jax.ShapeDtypeStruct((samples, LANES), jnp.int32),
        ),
        in_specs=[
            pl.BlockSpec((1, span), lambda i: (0, 0)),
            pl.BlockSpec((1, rows // LANES, LANES), lambda i: (i, 0, 0)),
            pl.BlockSpec((rows, pixels), lambda i: (i, 0)),
        ],
        out_specs=(
            pl.BlockSpec((rows, wide), lambda i: (i, 0)),
            pl.BlockSpec((rows, LANES), lambda i: (i, 0)),
        ),
        scratch_shapes=[
            pltpu.VMEM((TPHI, span), BF16),
            pltpu.VMEM((TR * span, LANES), BF16),
            pltpu.VMEM((LANES, wide), BF16),
        ],
        name="spread_samples",
        cost_estimate=pl.CostEstimate(
            flops=samples * wide * LANES * 4, bytes_accessed=samples * wide * 2, transcendentals=0
        ),
    )(order_lanes, code.reshape(steps, rows // LANES, LANES), interp)


def pick_kernel(count, x_ref, mark_ref, *refs):
    pieces, out_ref, table_ref = refs[:count], refs[count], refs[count + 1]
    rows = x_ref.shape[0]
    wide = table_ref.shape[0]
    dets = out_ref.shape[1]

    @pl.when(pl.program_id(0) == 0)
    def _():
        for j, piece in enumerate(pieces):
            table_ref[:, j * LANES : (j + 1) * LANES] = piece[...]

    sums = lax.dot_general(
        x_ref[...], table_ref[...], CONTRACT_LAST, preferred_element_type=F32
    )
    lane = iota((rows, LANES), 1)
    kept = []
    for block in range(wide // LANES):
        hit = mark_ref[...] == (lane + LANES * block) // dets
        kept.append(jnp.where(hit, sums[:, block * LANES : (block + 1) * LANES], 0.0))
    kept = jnp.concatenate(kept, axis=1).astype(BF16)
    gather = (iota((wide, dets), 0) % dets == iota((wide, dets), 1)).astype(F32).astype(BF16)
    out_ref[...] = jnp.dot(kept, gather, preferred_element_type=F32).astype(BF16)


def pick_values(x, mark, pieces, dets):
    samples, wide = x.shape
    rows = min(512, samples)
    count = len(pieces)
    table_rows = pieces[0].shape[0]
    whole = pl.BlockSpec((table_rows, LANES), lambda i: (0, 0))
    return pl.pallas_call(
        functools.partial(pick_kernel, count),
        grid=(samples // rows,),
        out_shape=jax.ShapeDtypeStruct((samples, dets), BF16),
        in_specs=[
            pl.BlockSpec((rows, wide), lambda i: (i, 0)),
            pl.BlockSpec((rows, LANES), lambda i: (i, 0)),
        ]
        + [whole] * count,
        out_specs=pl.BlockSpec((rows, dets), lambda i: (i, 0)),
        scratch_shapes=[pltpu.VMEM((table_rows, wide), BF16)],
        name="pick_values",
    )(x, mark, *pieces)


def gather_pieces(piece, group_count, sub_count):
    pieces = [piece]
    step = 1
    while step < group_count:
        swap = [(i, i ^ step) for i in range(group_count)]
        pieces = pieces + [lax.ppermute(p, "grp", swap) for p in pieces]
        step *= 2
    step = sub_count // 2
    while step:
        swap = [(i, i ^ step) for i in range(sub_count)]
        pieces = pieces + [lax.ppermute(p, "sub", swap) for p in pieces]
        step //= 2
    return pieces


def piece_slots(group_count, sub_count):
    slots = [(0, 0)]
    step = 1
    while step < group_count:
        slots = slots + [(g ^ step, s) for g, s in slots]
        step *= 2
    step = sub_count // 2
    while step:
        slots = slots + [(g, s ^ step) for g, s in slots]
        step //= 2
    return slots


def lanes_of(orders):
    return jnp.tile(jnp.repeat(orders, 2), NPHI // TPHI)[None, :]


def in_chunks(piece, orders, code, interp, dets):
    chunk = LANES // (2 * TR)
    chunks = orders.shape[0] // chunk
    gathered = lax.all_gather(piece, ("grp", "sub"), axis=0)
    gathered = gathered.reshape(chunks, chunk, piece.shape[0], LANES)

    def add_chunk(member, sums):
        x, _ = spread_samples(
            lanes_of(lax.dynamic_slice_in_dim(orders, member * chunk, chunk)), code, interp
        )
        table = lax.dynamic_index_in_dim(gathered, member, 0, False)
        table = table.transpose(0, 2, 1).reshape(chunk * LANES, piece.shape[0])
        return sums + jnp.dot(x, table, preferred_element_type=F32)

    samples = interp.shape[0]
    sums = lax.fori_loop(0, chunks, add_chunk, jnp.zeros((samples, piece.shape[0]), F32))
    mark = code // ((NPHI // TPHI) * chunk)
    hit = mark[:, None] == lax.iota(jnp.int32, piece.shape[0] // dets)[None, :]
    sums = sums.reshape(samples, piece.shape[0] // dets, dets)
    return jnp.sum(jnp.where(hit[:, :, None], sums, 0.0), axis=1).astype(BF16)


def on_device(alm, band_index, band_weight, legendre, orders, owner, tile_local, interp):
    group_count = lax.axis_size("grp")
    sub_count = lax.axis_size("sub")
    local_freqs = alm.shape[0]
    multipoles = alm.shape[3]
    cycles = legendre.shape[2]
    dets = band_weight.shape[0] // lax.axis_size("freq")
    samples = interp.shape[0]
    parts = LANES // TR
    group, sub = lax.axis_index("grp"), lax.axis_index("sub")
    my_slot = group * sub_count + sub

    own, send = band_sums(band_index, band_weight, alm.reshape(2 * local_freqs, multipoles))
    received = lax.ppermute(send, "freq", [(0, 1), (1, 0)])

    tiles_each = (cycles // (group_count * sub_count) // TR) * (NPHI // TPHI)
    code = owner[:, 0] * tiles_each + tile_local
    piece = cycle_coefs(orders[my_slot][None], own, received, legendre[0])
    if orders.shape[0] == parts // 2:
        offsets = piece_slots(group_count, sub_count)
        slots = (group ^ jnp.array([g for g, _ in offsets], jnp.int32)) * sub_count + (
            sub ^ jnp.array([s for _, s in offsets], jnp.int32)
        )
        x, mark = spread_samples(lanes_of(orders[slots]), code, interp)
        pieces = gather_pieces(piece, group_count, sub_count)
        return pick_values(x, mark, pieces, dets)
    return in_chunks(piece, orders, code, interp, dets)


def solution(mesh):
    placed = (
        P("freq", ("grp", "sub"), None, None),
        P(),
        P(),
        P(("grp", "sub"), None, None),
        P(),
        P(("grp", "sub"), None),
        P(("grp", "sub")),
        P(("grp", "sub"), None),
    )
    return jax.shard_map(
        on_device, mesh=mesh, in_specs=placed, out_specs=P(("grp", "sub"), "freq"), check_vma=False
    )
```

```python
import functools
import math

import jax
import jax.numpy as jnp
from jax import lax
from jax.experimental import pallas as pl
from jax.experimental.pallas import tpu as pltpu
from jax.sharding import PartitionSpec as P

NPHI = 1024
TR = 4
TPHI = 128
LANES = 128
LOWS = LANES // (2 * TR)
FOLD = 4
F32 = jnp.float32
BF16 = jnp.bfloat16
CONTRACT_LAST = (((1,), (1,)), ((), ()))


def iota(shape, axis):
    return lax.broadcasted_iota(jnp.int32, shape, axis)


def band_kernel(index_ref, weight_ref, alm_ref, own_ref, send_ref):
    rows = alm_ref.shape[0]
    dets, entries = index_ref.shape
    half = dets // 2
    me = lax.axis_index("freq")
    column = iota((dets, rows), 1)
    wanted = me * (rows // 2) + lax.shift_right_logical(column, 1)
    band = jnp.zeros((dets, rows), F32)
    for k in range(entries):
        hit = index_ref[:, k : k + 1] == wanted
        band = band + jnp.where(hit, weight_ref[:, k : k + 1], 0.0)
    part = lax.bitwise_and(column[:half], 1)
    low, high = band[:half], band[half:]
    own = jnp.where(me == 0, low, high)
    other = jnp.where(me == 0, high, low)
    matrix = jnp.concatenate(
        [jnp.where(part == c, side, 0.0) for side in (own, other) for c in range(2)]
    ).astype(BF16)
    sums = jnp.dot(matrix, alm_ref[...], preferred_element_type=F32)
    own_ref[...] = sums[:dets]
    send_ref[...] = sums[dets:].astype(BF16)


def band_sums(band_index, band_weight, alm):
    rows, multipoles = alm.shape
    dets = band_index.shape[0]
    return pl.pallas_call(
        band_kernel,
        out_shape=(
            jax.ShapeDtypeStruct((dets, multipoles), F32),
            jax.ShapeDtypeStruct((dets, multipoles), BF16),
        ),
        name="band_sums",
    )(band_index, band_weight, alm)


def cycle_kernel(order_ref, own_ref, recv_ref, legendre_ref, out_ref):
    rows, multipoles = own_ref.shape
    half = rows // 2
    cycles = legendre_ref.shape[1]
    keep = iota((rows, multipoles), 1) >= order_ref[0]
    coefs = own_ref[...] + recv_ref[...].astype(F32)
    coefs = jnp.where(keep, coefs, 0.0).astype(BF16)
    table = jnp.dot(coefs, legendre_ref[...], preferred_element_type=F32)
    first = iota((half, LANES), 1) < LANES // 2
    lines = []
    for tile in range(cycles // LANES):
        both = table[:, tile * LANES : (tile + 1) * LANES]
        turned = pltpu.roll(both, LANES // 2, 1)
        lines.append(jnp.where(first, both[:half], turned[half:]))
        lines.append(jnp.where(first, turned[:half], both[half:]))
    each = LANES // half
    for block in range(len(lines) // each):
        square = jnp.concatenate(lines[block * each : (block + 1) * each])
        out_ref[:, block * LANES : (block + 1) * LANES] = square.T.astype(BF16)


def cycle_coefs(order, own, received, legendre):
    rows, multipoles = own.shape
    cycles = legendre.shape[1]
    return pl.pallas_call(
        cycle_kernel,
        out_shape=jax.ShapeDtypeStruct((LANES, rows * cycles // LANES), BF16),
        in_specs=[pl.BlockSpec(memory_space=pltpu.SMEM)]
        + [pl.BlockSpec(memory_space=pltpu.VMEM)] * 3,
        name="cycle_coefs",
    )(order, own, received, legendre)


def spread_kernel(orders_ref, code_ref, interp_ref, x_ref, low_ref, high_ref, base_ref, turn_ref, copy_ref):
    rows, pixels = interp_ref.shape
    parts = LANES // TR
    lon_tiles = NPHI // TPHI

    @pl.when(pl.program_id(0) == 0)
    def _():
        order = jnp.broadcast_to(orders_ref[...], (TPHI, 2 * LANES))
        place = iota((TPHI, 2 * LANES), 0)
        lane = iota((TPHI, 2 * LANES), 1)
        side = lane // LANES
        turns = order * place + (NPHI // 4) * (side + lane % 2)
        angle = lax.bitwise_and(turns, NPHI - 1).astype(F32) * (2.0 * math.pi / NPHI)
        base = jnp.where(order == 0, 1.0, 2.0) * jnp.cos(angle)
        for i in range(TR):
            held = jnp.where((lane % LANES) // parts == i, base, 0.0)
            base_ref[i * TPHI : (i + 1) * TPHI, :] = held.astype(BF16)
        turns = order * (place % lon_tiles) * TPHI + 3 * (NPHI // 4) * side
        angle = lax.bitwise_and(turns, NPHI - 1).astype(F32) * (2.0 * math.pi / NPHI)
        turn = jnp.cos(angle)
        rounded = turn.astype(BF16).astype(F32)
        turn = jnp.where(place < lon_tiles, rounded, turn - rounded)
        turn_ref[...] = jnp.where(place < 2 * lon_tiles, turn, 0.0).astype(BF16)
        row = iota((LANES, FOLD * LANES), 0)
        lane = iota((LANES, FOLD * LANES), 1)
        hit = (row // parts == lane % TR) & (row % parts == lane // (FOLD * TR))
        copy_ref[...] = jnp.where(hit, 1.0, 0.0).astype(BF16)

    groups = []
    for group in range(rows // LANES):
        line = code_ref[0, group : group + 1, :].astype(F32)
        groups.append(jnp.broadcast_to(line, (LANES, LANES)).T)
    code = jnp.concatenate(groups).astype(jnp.int32)
    lane = iota((rows, LANES), 1)
    lon_tile = lax.bitwise_and(code, lon_tiles - 1)
    cycle_tile = lax.shift_right_logical(code, lon_tiles.bit_length() - 1)
    low = lax.bitwise_and(cycle_tile, LOWS - 1)
    low_ref[...] = (low - (lane // TR) % FOLD).astype(F32).astype(BF16)
    high = lax.shift_right_logical(cycle_tile, LOWS.bit_length() - 1)
    high_ref[...] = high.astype(F32).astype(BF16)
    tile_hit = (lane < 2 * lon_tiles) & (lane % lon_tiles == lon_tile)
    tile_hit = jnp.where(tile_hit, 1.0, 0.0).astype(BF16)
    turn = jnp.dot(tile_hit, turn_ref[...], preferred_element_type=F32)
    pair = jnp.dot(interp_ref[...], base_ref[...], preferred_element_type=F32) * turn
    both = (pair[:, :LANES] + pair[:, LANES:]).astype(BF16)
    x_ref[...] = jnp.dot(both, copy_ref[...], preferred_element_type=F32).astype(BF16)


def spread_samples(order_lanes, code, interp):
    samples, pixels = interp.shape
    rows = min(512, samples)
    steps = samples // rows
    return pl.pallas_call(
        spread_kernel,
        grid=(steps,),
        out_shape=(
            jax.ShapeDtypeStruct((samples, FOLD * LANES), BF16),
            jax.ShapeDtypeStruct((samples, LANES), BF16),
            jax.ShapeDtypeStruct((samples, LANES), BF16),
        ),
        in_specs=[
            pl.BlockSpec((1, 2 * LANES), lambda i: (0, 0)),
            pl.BlockSpec((1, rows // LANES, LANES), lambda i: (i, 0, 0)),
            pl.BlockSpec((rows, pixels), lambda i: (i, 0)),
        ],
        out_specs=(
            pl.BlockSpec((rows, FOLD * LANES), lambda i: (i, 0)),
            pl.BlockSpec((rows, LANES), lambda i: (i, 0)),
            pl.BlockSpec((rows, LANES), lambda i: (i, 0)),
        ),
        scratch_shapes=[
            pltpu.VMEM((pixels, 2 * LANES), BF16),
            pltpu.VMEM((LANES, 2 * LANES), BF16),
            pltpu.VMEM((LANES, FOLD * LANES), BF16),
        ],
        name="spread_samples",
        cost_estimate=pl.CostEstimate(
            flops=samples * pixels * LANES * 16,
            bytes_accessed=samples * pixels * 4,
            transcendentals=0,
        ),
    )(order_lanes, code.reshape(steps, rows // LANES, LANES), interp)


def pick_kernel(count, x_ref, low_ref, high_ref, *refs):
    pieces, out_ref, table_ref = refs[:count], refs[count], refs[count + 1]
    dets, rows = out_ref.shape
    wide = table_ref.shape[2]
    tile = FOLD * TR

    @pl.when(pl.program_id(0) == 0)
    def _():
        for j, piece in enumerate(pieces):
            for c in range(2):
                for q in range(LOWS // FOLD):
                    table_ref[q, pl.ds((2 * j + c) * tile, tile), :] = piece[
                        pl.ds((c * LOWS // FOLD + q) * tile, tile), :
                    ]

    zero = jnp.zeros((rows, LANES), BF16)
    sums = jnp.zeros((rows, wide), F32)
    for q in range(LOWS // FOLD):
        hit = low_ref[...] == jnp.asarray(FOLD * q, BF16)
        cut = [
            jnp.where(hit, x_ref[:, b * LANES : (b + 1) * LANES], zero) for b in range(FOLD)
        ]
        sums = sums + jnp.dot(
            jnp.concatenate(cut, axis=1), table_ref[q], preferred_element_type=F32
        )
    sums = sums.astype(BF16)
    kept = []
    for b in range(wide // LANES):
        lane = ((iota((rows, LANES), 1) + LANES * b) // dets).astype(F32).astype(BF16)
        kept.append(jnp.where(high_ref[...] == lane, sums[:, b * LANES : (b + 1) * LANES], zero))
    gather = iota((dets, wide), 1) % dets == iota((dets, wide), 0)
    gather = jnp.where(gather, 1.0, 0.0).astype(BF16)
    out_ref[...] = lax.dot_general(
        gather, jnp.concatenate(kept, axis=1), CONTRACT_LAST, preferred_element_type=F32
    ).astype(BF16)


def pick_values(x, low, high, pieces, dets):
    samples = x.shape[0]
    rows = min(1024, samples)
    count = len(pieces)
    table_lanes = pieces[0].shape[1]
    return pl.pallas_call(
        functools.partial(pick_kernel, count),
        grid=(samples // rows,),
        out_shape=jax.ShapeDtypeStruct((dets, samples), BF16),
        in_specs=[
            pl.BlockSpec((rows, FOLD * LANES), lambda i: (i, 0)),
            pl.BlockSpec((rows, LANES), lambda i: (i, 0)),
            pl.BlockSpec((rows, LANES), lambda i: (i, 0)),
        ]
        + [pl.BlockSpec((LANES, table_lanes), lambda i: (0, 0))] * count,
        out_specs=pl.BlockSpec((dets, rows), lambda i: (0, i)),
        scratch_shapes=[pltpu.VMEM((LOWS // FOLD, FOLD * LANES, table_lanes), BF16)],
        name="pick_values",
    )(x, low, high, *pieces)


def gather_pieces(piece, group_count, sub_count):
    pieces = [piece]
    step = 1
    while step < group_count:
        swap = [(i, i ^ step) for i in range(group_count)]
        pieces = pieces + [lax.ppermute(p, "grp", swap) for p in pieces]
        step *= 2
    step = sub_count // 2
    while step:
        swap = [(i, i ^ step) for i in range(sub_count)]
        pieces = pieces + [lax.ppermute(p, "sub", swap) for p in pieces]
        step //= 2
    return pieces


def piece_slots(group_count, sub_count):
    slots = [(0, 0)]
    step = 1
    while step < group_count:
        slots = slots + [(g ^ step, s) for g, s in slots]
        step *= 2
    step = sub_count // 2
    while step:
        slots = slots + [(g, s ^ step) for g, s in slots]
        step //= 2
    return slots


def lanes_of(orders):
    return jnp.tile(jnp.repeat(orders, 2), 2 * TR)[None, :]


def in_chunks(piece, orders, code, interp, dets):
    chunks = orders.shape[0] // LOWS
    lanes = piece.shape[1]
    steps = LOWS // FOLD
    gathered = lax.all_gather(piece, ("grp", "sub"), axis=0)
    gathered = gathered.reshape(chunks, LOWS, 2, steps, FOLD * TR, lanes)

    def add_chunk(member, sums):
        x, low, _ = spread_samples(
            lanes_of(lax.dynamic_slice_in_dim(orders, member * LOWS, LOWS)), code, interp
        )
        table = lax.dynamic_index_in_dim(gathered, member, 0, False)
        table = table.transpose(2, 0, 1, 3, 4).reshape(steps, FOLD * LANES, lanes)
        for q in range(steps):
            hit = jnp.tile(low == FOLD * q, (1, FOLD))
            cut = jnp.where(hit, x, jnp.zeros_like(x))
            sums = sums + jnp.dot(cut, table[q], preferred_element_type=F32)
        return sums

    samples = interp.shape[0]
    sums = lax.fori_loop(0, chunks, add_chunk, jnp.zeros((samples, lanes), F32))
    mark = code // ((NPHI // TPHI) * LOWS)
    hit = mark[:, None] == lax.iota(jnp.int32, lanes // dets)[None, :]
    sums = sums.reshape(samples, lanes // dets, dets)
    return jnp.sum(jnp.where(hit[:, :, None], sums, 0.0), axis=1).astype(BF16)


def on_device(alm, band_index, band_weight, legendre, orders, owner, tile_local, interp):
    group_count = lax.axis_size("grp")
    sub_count = lax.axis_size("sub")
    local_freqs = alm.shape[0]
    multipoles = alm.shape[3]
    cycles = legendre.shape[2]
    dets = band_weight.shape[0] // lax.axis_size("freq")
    samples = interp.shape[0]
    group, sub = lax.axis_index("grp"), lax.axis_index("sub")
    my_slot = group * sub_count + sub

    own, send = band_sums(band_index, band_weight, alm.reshape(2 * local_freqs, multipoles))
    received = lax.ppermute(send, "freq", [(0, 1), (1, 0)])

    tiles_each = (cycles // (group_count * sub_count) // TR) * (NPHI // TPHI)
    code = owner[:, 0] * tiles_each + tile_local
    piece = cycle_coefs(orders[my_slot][None], own, received, legendre[0])
    if orders.shape[0] == LOWS:
        offsets = piece_slots(group_count, sub_count)
        slots = (group ^ jnp.array([g for g, _ in offsets], jnp.int32)) * sub_count + (
            sub ^ jnp.array([s for _, s in offsets], jnp.int32)
        )
        x, low, high = spread_samples(lanes_of(orders[slots]), code, interp)
        pieces = gather_pieces(piece, group_count, sub_count)
        return pick_values(x, low, high, pieces, dets).T
    return in_chunks(piece, orders, code, interp, dets)


def solution(mesh):
    placed = (
        P("freq", ("grp", "sub"), None, None),
        P(),
        P(),
        P(("grp", "sub"), None, None),
        P(),
        P(("grp", "sub"), None),
        P(("grp", "sub")),
        P(("grp", "sub"), None),
    )
    return jax.shard_map(
        on_device, mesh=mesh, in_specs=placed, out_specs=P(("grp", "sub"), "freq"), check_vma=False
    )
```

```python
import functools
import math

import jax
import jax.numpy as jnp
from jax import lax
from jax.experimental import pallas as pl
from jax.experimental.pallas import tpu as pltpu
from jax.sharding import PartitionSpec as P

NPHI = 1024
TR = 4
TPHI = 128
LANES = 128
LOWS = LANES // (2 * TR)
FOLD = 4
SMALL = 12 * 2**20
F32 = jnp.float32
BF16 = jnp.bfloat16
CONTRACT_LAST = (((1,), (1,)), ((), ()))


def iota(shape, axis):
    return lax.broadcasted_iota(jnp.int32, shape, axis)


def in_hbm(value):
    return pltpu.with_memory_space_constraint(value, pltpu.HBM)


def band_kernel(
    index_ref, weight_ref, orders_ref, alm_ref, own_ref, send_ref, index, weight, orders, alm, sem
):
    sources = (index_ref, weight_ref, orders_ref, alm_ref)
    copies = [
        pltpu.make_async_copy(source, target, sem.at[n])
        for n, (source, target) in enumerate(zip(sources, (index, weight, orders, alm)))
    ]
    for copy in copies:
        copy.start()
    freqs, _, multipoles = alm.shape
    rows = 2 * freqs
    dets, entries = index.shape
    half = dets // 2
    me = lax.axis_index("freq")
    slot = lax.axis_index("grp") * lax.axis_size("sub") + lax.axis_index("sub")
    column = iota((dets, rows), 1)
    wanted = me * freqs + lax.shift_right_logical(column, 1)
    band = jnp.zeros((dets, rows), F32)
    copies[0].wait()
    copies[1].wait()
    for k in range(entries):
        hit = index[:, k : k + 1] == wanted
        band = band + jnp.where(hit, weight[:, k : k + 1], 0.0)
    part = lax.bitwise_and(column[:half], 1)
    low, high = band[:half], band[half:]
    own = jnp.where(me == 0, low, high)
    other = jnp.where(me == 0, high, low)
    matrix = jnp.concatenate(
        [jnp.where(part == c, side, 0.0) for side in (own, other) for c in range(2)]
    ).astype(BF16)
    copies[2].wait()
    keep = iota((dets, multipoles), 1) >= orders[slot]
    copies[3].wait()
    table = alm[...].reshape(rows, multipoles)
    sums = jnp.dot(matrix, table, preferred_element_type=F32)
    own_ref[...] = jnp.where(keep, sums[:dets], 0.0)
    send_ref[...] = jnp.where(keep, sums[dets:], 0.0).astype(BF16)


def band_sums(band_index, band_weight, orders, alm):
    multipoles = alm.shape[2]
    dets = band_index.shape[0]
    return pl.pallas_call(
        band_kernel,
        out_shape=(
            jax.ShapeDtypeStruct((dets, multipoles), F32),
            jax.ShapeDtypeStruct((dets, multipoles), BF16),
        ),
        in_specs=[pl.BlockSpec(memory_space=pltpu.HBM)] * 4,
        scratch_shapes=[
            pltpu.VMEM(band_index.shape, jnp.int32),
            pltpu.VMEM(band_weight.shape, F32),
            pltpu.SMEM(orders.shape, jnp.int32),
            pltpu.VMEM(alm.shape, BF16),
            pltpu.SemaphoreType.DMA((4,)),
        ],
        compiler_params=pltpu.CompilerParams(vmem_limit_bytes=SMALL),
        name="band_sums",
    )(*[in_hbm(value) for value in (band_index, band_weight, orders, alm)])


def cycle_kernel(own_ref, recv_ref, legendre_ref, out_ref):
    rows = own_ref.shape[0]
    half = rows // 2
    cycles = legendre_ref.shape[1]
    coefs = (own_ref[...] + recv_ref[...].astype(F32)).astype(BF16)
    table = jnp.dot(coefs, legendre_ref[...], preferred_element_type=F32)
    first = iota((half, LANES), 1) < LANES // 2
    lines = []
    for tile in range(cycles // LANES):
        both = table[:, tile * LANES : (tile + 1) * LANES]
        turned = pltpu.roll(both, LANES // 2, 1)
        lines.append(jnp.where(first, both[:half], turned[half:]))
        lines.append(jnp.where(first, turned[:half], both[half:]))
    each = LANES // half
    for block in range(len(lines) // each):
        square = jnp.concatenate(lines[block * each : (block + 1) * each])
        out_ref[:, block * LANES : (block + 1) * LANES] = square.T.astype(BF16)


def cycle_coefs(own, received, legendre):
    rows, multipoles = own.shape
    cycles = legendre.shape[1]
    return pl.pallas_call(
        cycle_kernel,
        out_shape=jax.ShapeDtypeStruct((LANES, rows * cycles // LANES), BF16),
        in_specs=[pl.BlockSpec(memory_space=pltpu.VMEM)] * 3,
        compiler_params=pltpu.CompilerParams(vmem_limit_bytes=SMALL),
        name="cycle_coefs",
    )(own, received, legendre)


def copy_table(first_row):
    parts = LANES // 2 // TR
    row = iota((LANES, FOLD * LANES // 2), 0) - first_row
    lane = iota((LANES, FOLD * LANES // 2), 1)
    hit = (row >= 0) & (row < LANES // 2)
    hit = hit & (row // parts == lane % TR) & (row % parts == lane // (FOLD * TR))
    return jnp.where(hit, 1.0, 0.0).astype(BF16)


def column_of(line):
    return jnp.broadcast_to(line.astype(F32), (LANES, LANES)).T


def lane_bits(rows):
    return (iota((rows, LANES), 1) // TR) % FOLD


def spread_kernel(
    tiles_each, slots, first_ref, orders_hbm, owner_hbm, tile_hbm, interp_hbm,
    x_ref, low_ref, high_ref, packet_ref, base_ref, turn_ref,
    orders_ref, owner_ref, tile_ref, interp_ref, sem
):
    samples, pixels = interp_ref.shape
    lon_tiles = NPHI // TPHI
    rows = min(512, samples)
    pairs = [(orders_hbm, orders_ref), (owner_hbm, owner_ref), (tile_hbm, tile_ref)]
    for step in range(samples // rows):
        here = pl.ds(step * rows, rows)
        pairs.append((interp_hbm.at[here, :], interp_ref.at[here, :]))
    copies = [
        pltpu.make_async_copy(source, target, sem.at[n])
        for n, (source, target) in enumerate(pairs)
    ]
    for fetch in copies:
        fetch.start()
    copies[0].wait()

    place = iota((TPHI, 2 * LANES), 0)
    lane = iota((TPHI, 2 * LANES), 1)
    side = lane // LANES
    held = lane % (LANES // 2 // TR) // 2 + LOWS // 2 * (lane % LANES // (LANES // 2))
    order = jnp.zeros((TPHI, 2 * LANES), jnp.int32)
    for j, slot in enumerate(slots(first_ref[0])):
        order = jnp.where(held == j, orders_ref[slot], order)
    turns = order * place + (NPHI // 4) * (side + lane % 2)
    angle = lax.bitwise_and(turns, NPHI - 1).astype(F32) * (2.0 * math.pi / NPHI)
    base = jnp.where(order == 0, 1.0, 2.0) * jnp.cos(angle)
    for i in range(TR):
        kept = jnp.where(lane % (LANES // 2) // (LANES // 2 // TR) == i, base, 0.0)
        base_ref[i * TPHI : (i + 1) * TPHI, :] = kept.astype(BF16)
    turns = order * (place % lon_tiles) * TPHI + 3 * (NPHI // 4) * side
    angle = lax.bitwise_and(turns, NPHI - 1).astype(F32) * (2.0 * math.pi / NPHI)
    turn = jnp.cos(angle)
    rounded = turn.astype(BF16).astype(F32)
    turn = jnp.where(place < lon_tiles, rounded, turn - rounded)
    turn_ref[...] = jnp.where(place < 2 * lon_tiles, turn, 0.0).astype(BF16)
    copy = copy_table(0)

    copies[1].wait()
    copies[2].wait()
    code = owner_ref[...] * tiles_each + tile_ref[...]
    cycle_tile = lax.shift_right_logical(code, lon_tiles.bit_length() - 1)
    lon_tile = lax.bitwise_and(code, lon_tiles - 1)
    low = lax.bitwise_and(cycle_tile, LOWS - 1)
    high = lax.shift_right_logical(cycle_tile, LOWS.bit_length() - 1)
    lines = samples // LANES
    packet_ref[samples // 2 : samples // 2 + lines, :] = low.astype(F32).astype(BF16)
    packet_ref[samples // 2 + lines :, :] = high.astype(F32).astype(BF16)

    lane = iota((rows, LANES), 1)
    far_first = []
    for step in range(samples // rows):
        here = slice(step * rows, (step + 1) * rows)
        groups = range(step * rows // LANES, (step + 1) * rows // LANES)
        columns = jnp.concatenate([column_of(code[g : g + 1, :]) for g in groups])
        columns = columns.astype(jnp.int32)
        lon_tile = lax.bitwise_and(columns, lon_tiles - 1)
        cycle_tile = lax.shift_right_logical(columns, lon_tiles.bit_length() - 1)
        low = lax.bitwise_and(cycle_tile, LOWS - 1)
        low_ref[here, :] = (low - lane_bits(rows)).astype(F32).astype(BF16)
        high = lax.shift_right_logical(cycle_tile, LOWS.bit_length() - 1)
        high_ref[here, :] = high.astype(F32).astype(BF16)
        tile_hit = (lane < 2 * lon_tiles) & (lane % lon_tiles == lon_tile)
        tile_hit = jnp.where(tile_hit, 1.0, 0.0).astype(BF16)
        turn = jnp.dot(tile_hit, turn_ref[...], preferred_element_type=F32)
        copies[3 + step].wait()
        pair = jnp.dot(interp_ref[here, :], base_ref[...], preferred_element_type=F32) * turn
        both = pair[:, :LANES] + pair[:, LANES:]
        x_ref[here, :] = jnp.dot(both.astype(BF16), copy, preferred_element_type=F32).astype(BF16)
        if step < samples // rows // 2:
            far_first.append(pltpu.roll(both, LANES // 2, 1))
        else:
            step -= samples // rows // 2
            packed = jnp.where(lane < LANES // 2, far_first[step], both)
            packet_ref[step * rows : (step + 1) * rows, :] = packed.astype(BF16)


def spread_samples(slots, first, orders, owner, tile, tiles_each, interp):
    samples, pixels = interp.shape
    lines = (samples // LANES, LANES)
    return pl.pallas_call(
        functools.partial(spread_kernel, tiles_each, slots),
        out_shape=(
            jax.ShapeDtypeStruct((samples, FOLD * LANES // 2), BF16),
            jax.ShapeDtypeStruct((samples, LANES), BF16),
            jax.ShapeDtypeStruct((samples, LANES), BF16),
            jax.ShapeDtypeStruct((samples // 2 + 2 * lines[0], LANES), BF16),
        ),
        in_specs=[pl.BlockSpec(memory_space=pltpu.SMEM)]
        + [pl.BlockSpec(memory_space=pltpu.HBM)] * 4,
        scratch_shapes=[
            pltpu.VMEM((pixels, 2 * LANES), BF16),
            pltpu.VMEM((LANES, 2 * LANES), BF16),
            pltpu.SMEM(orders.shape, jnp.int32),
            pltpu.VMEM(lines, jnp.int32),
            pltpu.VMEM(lines, jnp.int32),
            pltpu.VMEM((samples, pixels), BF16),
            pltpu.SemaphoreType.DMA((3 + samples // min(512, samples),)),
        ],
        compiler_params=pltpu.CompilerParams(vmem_limit_bytes=SMALL),
        name="spread_samples",
        cost_estimate=pl.CostEstimate(
            flops=samples * pixels * LANES * 16,
            bytes_accessed=samples * pixels * 4,
            transcendentals=0,
        ),
    )(
        first,
        in_hbm(orders),
        in_hbm(owner.reshape(lines)),
        in_hbm(tile.reshape(lines)),
        in_hbm(interp),
    )


def unpack_kernel(packet_ref, x_ref, low_ref, high_ref):
    samples = x_ref.shape[0]
    lines = samples // LANES
    rows = min(512, samples // 2)
    half = samples // 2
    for side in range(2):
        copy = copy_table(side * LANES // 2)
        for step in range(half // rows):
            part = packet_ref[step * rows : (step + 1) * rows, :]
            spread = jnp.dot(part, copy, preferred_element_type=F32)
            x_ref[side * half + step * rows : side * half + (step + 1) * rows, :] = spread.astype(BF16)
    low = packet_ref[half : half + lines, :].astype(F32)
    high = packet_ref[half + lines :, :].astype(F32)
    bits = lane_bits(LANES).astype(F32)
    for g in range(lines):
        here = slice(g * LANES, (g + 1) * LANES)
        low_ref[here, :] = (column_of(low[g : g + 1, :]) - bits).astype(BF16)
        high_ref[here, :] = column_of(high[g : g + 1, :]).astype(BF16)


def unpack_samples(packet, samples):
    return pl.pallas_call(
        unpack_kernel,
        out_shape=(
            jax.ShapeDtypeStruct((samples, FOLD * LANES // 2), BF16),
            jax.ShapeDtypeStruct((samples, LANES), BF16),
            jax.ShapeDtypeStruct((samples, LANES), BF16),
        ),
        in_specs=[pl.BlockSpec(memory_space=pltpu.VMEM)],
        compiler_params=pltpu.CompilerParams(vmem_limit_bytes=SMALL),
        name="unpack_samples",
        cost_estimate=pl.CostEstimate(
            flops=samples * LANES * LANES * 8, bytes_accessed=samples * LANES * 8, transcendentals=0
        ),
    )(packet)


def pick_kernel(counts, first_block, more, last, x_ref, low_ref, high_ref, *refs):
    stacks, rest = refs[: len(counts)], refs[len(counts) :]
    sums_ref = rest[0] if more else None
    out_ref, table_ref = rest[-2], rest[-1]
    samples = x_ref.shape[0]
    wide = table_ref.shape[1]
    steps, tile = LOWS // FOLD, FOLD * TR
    blocks = sum(counts) // (LANES // (2 * tile))
    j = 0
    for stack, count in zip(stacks, counts):
        for k in range(count):
            for c in range(2):
                for q in range(steps):
                    table_ref[pl.ds(q * blocks * LANES + (2 * j + c) * tile, tile), :] = stack[
                        pl.ds(k * LANES + (c * steps + q) * tile, tile), :
                    ]
            j += 1

    rows = min(512, samples)
    zero = jnp.zeros((rows, LANES), BF16)
    for step in range(samples // rows):
        here = slice(step * rows, (step + 1) * rows)
        low = low_ref[here, :]
        cut = [
            jnp.where(
                low == jnp.asarray(FOLD * q, BF16),
                x_ref[here, (first_block + b) * LANES : (first_block + b + 1) * LANES],
                zero,
            )
            for q in range(steps)
            for b in range(blocks)
        ]
        sums = jnp.dot(
            jnp.concatenate(cut, axis=1), table_ref[...], preferred_element_type=F32
        )
        if more:
            sums = sums + sums_ref[here, :]
        if not last:
            out_ref[here, :] = sums
            continue
        dets = out_ref.shape[0]
        sums = sums.astype(BF16)
        kept = []
        for b in range(wide // LANES):
            lane = ((iota((rows, LANES), 1) + LANES * b) // dets).astype(F32).astype(BF16)
            hit = high_ref[here, :] == lane
            kept.append(jnp.where(hit, sums[:, b * LANES : (b + 1) * LANES], zero))
        gather = iota((dets, wide), 1) % dets == iota((dets, wide), 0)
        gather = jnp.where(gather, 1.0, 0.0).astype(BF16)
        out_ref[:, here] = lax.dot_general(
            gather, jnp.concatenate(kept, axis=1), CONTRACT_LAST, preferred_element_type=F32
        ).astype(BF16)


def pick_values(x, low, high, stacks, first, sums, dets):
    samples = x.shape[0]
    counts = tuple(stack.shape[0] // LANES for stack in stacks)
    wide = stacks[0].shape[1]
    more = [] if sums is None else [sums]
    operands = [x, low, high, *stacks, *more]
    shape = ((samples, wide), F32) if dets is None else ((dets, samples), BF16)
    return pl.pallas_call(
        functools.partial(
            pick_kernel, counts, first * 2 * FOLD * TR // LANES, bool(more), dets is not None
        ),
        out_shape=jax.ShapeDtypeStruct(*shape),
        in_specs=[pl.BlockSpec(memory_space=pltpu.VMEM)] * len(operands),
        scratch_shapes=[pltpu.VMEM((sum(counts) * LANES, wide), BF16)],
        compiler_params=pltpu.CompilerParams(vmem_limit_bytes=16 * 2**20),
        name="pick_values",
        cost_estimate=pl.CostEstimate(
            flops=samples * sum(counts) * LANES * wide * 2, bytes_accessed=samples * 2048, transcendentals=0
        ),
    )(*operands)


def swap(value, axis, step):
    size = lax.axis_size(axis)
    return lax.ppermute(value, axis, [(i, i ^ step) for i in range(size)])


def in_chunks(piece, orders, owner, tile, tiles_each, interp, dets):
    chunks = orders.shape[0] // LOWS
    lanes = piece.shape[1]
    steps = LOWS // FOLD
    samples = interp.shape[0]
    gathered = lax.all_gather(piece, ("grp", "sub"), axis=0)
    gathered = gathered.reshape(chunks, LOWS, 2, steps, FOLD * TR, lanes)

    def add_chunk(member, sums):
        x, low, _, packet = spread_samples(
            lambda first: [first + j for j in range(LOWS)],
            jnp.reshape(member * LOWS, (1,)),
            orders,
            owner,
            tile,
            tiles_each,
            interp,
        )
        x = jnp.concatenate([x, unpack_samples(packet, samples)[0]], axis=1)
        table = lax.dynamic_index_in_dim(gathered, member, 0, False)
        table = table.transpose(2, 0, 1, 3, 4).reshape(steps, FOLD * LANES, lanes)
        for q in range(steps):
            hit = jnp.tile(low == FOLD * q, (1, FOLD))
            cut = jnp.where(hit, x, jnp.zeros_like(x))
            sums = sums + jnp.dot(cut, table[q], preferred_element_type=F32)
        return sums

    sums = lax.fori_loop(0, chunks, add_chunk, jnp.zeros((samples, lanes), F32))
    mark = (owner * tiles_each + tile) // ((NPHI // TPHI) * LOWS)
    hit = mark[:, None] == lax.iota(jnp.int32, lanes // dets)[None, :]
    sums = sums.reshape(samples, lanes // dets, dets)
    return jnp.sum(jnp.where(hit[:, :, None], sums, 0.0), axis=1).astype(BF16)


def on_device(alm, band_index, band_weight, legendre, orders, owner, tile_local, interp):
    group_count = lax.axis_size("grp")
    sub_count = lax.axis_size("sub")
    local_freqs = alm.shape[0]
    multipoles = alm.shape[3]
    cycles = legendre.shape[2]
    dets = band_weight.shape[0] // lax.axis_size("freq")
    samples = interp.shape[0]
    group, sub = lax.axis_index("grp"), lax.axis_index("sub")

    own, send = band_sums(
        band_index, band_weight, orders, alm.reshape(local_freqs, 2, multipoles)
    )
    received = swap(send, "freq", 1)
    tiles_each = (cycles // (group_count * sub_count) // TR) * (NPHI // TPHI)
    owner = owner[:, 0]
    if orders.shape[0] != LOWS:
        piece = cycle_coefs(own, received, legendre[0])
        return in_chunks(piece, orders, owner, tile_local, tiles_each, interp, dets)

    far = sub_count // 2

    def slots(mine):
        return [
            (mine // sub_count ^ g) * sub_count + (mine % sub_count ^ s)
            for s in range(sub_count)
            for g in range(group_count)
        ]

    mine = jnp.reshape(group * sub_count + sub, (1,))
    x, low, high, packet = spread_samples(
        slots, mine, orders, owner, tile_local, tiles_each, interp
    )
    got = swap(packet, "sub", far)
    received, _ = lax.optimization_barrier((received, packet))
    piece = cycle_coefs(own, received, legendre[0])
    stack = jnp.concatenate([piece] + [swap(piece, "grp", g) for g in range(1, group_count)])
    stacks = [stack] + [swap(stack, "sub", s) for s in range(1, far)]
    far_x, far_low, far_high = unpack_samples(got, samples)
    sums = pick_values(far_x, far_low, far_high, stacks[:1], 0, None, None)
    far_values = pick_values(far_x, far_low, far_high, stacks[1:], group_count, sums, dets)
    other = swap(far_values, "sub", far)
    values = pick_values(x, low, high, stacks, 0, None, dets)
    return (values.astype(F32) + other.astype(F32)).astype(BF16).T


def solution(mesh):
    placed = (
        P("freq", ("grp", "sub"), None, None),
        P(),
        P(),
        P(("grp", "sub"), None, None),
        P(),
        P(("grp", "sub"), None),
        P(("grp", "sub")),
        P(("grp", "sub"), None),
    )
    return jax.shard_map(
        on_device, mesh=mesh, in_specs=placed, out_specs=P(("grp", "sub"), "freq"), check_vma=False
    )
```

```python
import functools
import math

import jax
import jax.numpy as jnp
from jax import lax
from jax.experimental import pallas as pl
from jax.experimental.pallas import tpu as pltpu
from jax.sharding import PartitionSpec as P


NPHI = 1024
TR = 4
TPHI = 128
LANES = 128
LOWS = LANES // (2 * TR)
FOLD = 4
SMALL = 12 * 2**20
F32 = jnp.float32
BF16 = jnp.bfloat16
CONTRACT_LAST = (((1,), (1,)), ((), ()))


def iota(shape, axis):
    return lax.broadcasted_iota(jnp.int32, shape, axis)


def in_hbm(value):
    return pltpu.with_memory_space_constraint(value, pltpu.HBM)


def band_kernel(
    tiles_each, slots,
    index_ref, weight_ref, orders_ref, owner_ref, tile_ref, alm_ref,
    own_ref, send_ref, lanes_ref, code_ref,
    index, weight, orders, owner, tile, alm, sem
):
    sources = (index_ref, weight_ref, orders_ref, alm_ref, owner_ref, tile_ref)
    copies = [
        pltpu.make_async_copy(source, target, sem.at[n])
        for n, (source, target) in enumerate(zip(sources, (index, weight, orders, alm, owner, tile)))
    ]
    for copy in copies:
        copy.start()
    freqs, _, multipoles = alm.shape
    rows = 2 * freqs
    dets, entries = index.shape
    half = dets // 2
    me = lax.axis_index("freq")
    slot = lax.axis_index("grp") * lax.axis_size("sub") + lax.axis_index("sub")
    column = iota((dets, rows), 1)
    wanted = me * freqs + lax.shift_right_logical(column, 1)
    band = jnp.zeros((dets, rows), F32)
    copies[0].wait()
    copies[1].wait()
    for k in range(entries):
        hit = index[:, k : k + 1] == wanted
        band = band + jnp.where(hit, weight[:, k : k + 1], 0.0)
    part = lax.bitwise_and(column[:half], 1)
    low, high = band[:half], band[half:]
    own = jnp.where(me == 0, low, high)
    other = jnp.where(me == 0, high, low)
    matrix = jnp.concatenate(
        [jnp.where(part == c, side, 0.0) for side in (own, other) for c in range(2)]
    ).astype(BF16)
    copies[2].wait()
    keep = iota((dets, multipoles), 1) >= orders[slot]
    lane = iota(lanes_ref.shape, 1)
    held = lane_order(lane)
    order = jnp.zeros(lanes_ref.shape, jnp.int32)
    for j, here in enumerate(slots(slot)):
        order = jnp.where(held == j, orders[here], order)
    lanes_ref[...] = order
    copies[4].wait()
    copies[5].wait()
    code_ref[...] = owner[...] * tiles_each + tile[...]
    copies[3].wait()
    table = alm[...].reshape(rows, multipoles)
    sums = jnp.dot(matrix, table, preferred_element_type=F32)
    own_ref[...] = jnp.where(keep, sums[:dets], 0.0)
    send_ref[...] = jnp.where(keep, sums[dets:], 0.0).astype(BF16)


def lane_order(lane):
    half = LANES // 2
    return lane % (half // TR) // 2 + LOWS // 2 * (lane % LANES // half)


def band_sums(band_index, band_weight, orders, owner, tile, alm, tiles_each, slots):
    multipoles = alm.shape[2]
    dets = band_index.shape[0]
    lines = (owner.shape[0] // LANES, LANES)
    operands = (band_index, band_weight, orders, owner.reshape(lines), tile.reshape(lines), alm)
    return pl.pallas_call(
        functools.partial(band_kernel, tiles_each, slots),
        out_shape=(
            jax.ShapeDtypeStruct((dets, multipoles), F32),
            jax.ShapeDtypeStruct((dets, multipoles), BF16),
            jax.ShapeDtypeStruct((8, 2 * LANES), jnp.int32),
            jax.ShapeDtypeStruct(lines, jnp.int32),
        ),
        in_specs=[pl.BlockSpec(memory_space=pltpu.HBM)] * len(operands),
        scratch_shapes=[
            pltpu.VMEM(band_index.shape, jnp.int32),
            pltpu.VMEM(band_weight.shape, F32),
            pltpu.SMEM(orders.shape, jnp.int32),
            pltpu.VMEM(lines, jnp.int32),
            pltpu.VMEM(lines, jnp.int32),
            pltpu.VMEM(alm.shape, BF16),
            pltpu.SemaphoreType.DMA((len(operands),)),
        ],
        compiler_params=pltpu.CompilerParams(vmem_limit_bytes=SMALL),
        name="band_sums",
    )(*[in_hbm(value) for value in operands])


def cycle_kernel(own_ref, recv_ref, legendre_ref, out_ref):
    rows = own_ref.shape[0]
    half = rows // 2
    cycles = legendre_ref.shape[1]
    coefs = (own_ref[...] + recv_ref[...].astype(F32)).astype(BF16)
    table = jnp.dot(coefs, legendre_ref[...], preferred_element_type=F32)
    first = iota((half, LANES), 1) < LANES // 2
    lines = []
    for tile in range(cycles // LANES):
        both = table[:, tile * LANES : (tile + 1) * LANES]
        turned = pltpu.roll(both, LANES // 2, 1)
        lines.append(jnp.where(first, both[:half], turned[half:]))
        lines.append(jnp.where(first, turned[:half], both[half:]))
    each = LANES // half
    for block in range(len(lines) // each):
        square = jnp.concatenate(lines[block * each : (block + 1) * each])
        out_ref[:, block * LANES : (block + 1) * LANES] = square.T.astype(BF16)


def cycle_coefs(own, received, legendre):
    rows, _ = own.shape
    cycles = legendre.shape[1]
    return pl.pallas_call(
        cycle_kernel,
        out_shape=jax.ShapeDtypeStruct((LANES, rows * cycles // LANES), BF16),
        in_specs=[pl.BlockSpec(memory_space=pltpu.VMEM)] * 3,
        compiler_params=pltpu.CompilerParams(vmem_limit_bytes=SMALL),
        name="cycle_coefs",
    )(own, received, legendre)


def copy_table(first_row):
    parts = LANES // 2 // TR
    row = iota((LANES, FOLD * LANES // 2), 0) - first_row
    lane = iota((LANES, FOLD * LANES // 2), 1)
    hit = (row >= 0) & (row < LANES // 2)
    hit = hit & (row // parts == lane % TR) & (row % parts == lane // (FOLD * TR))
    return jnp.where(hit, 1.0, 0.0).astype(BF16)


def column_of(line):
    return jnp.broadcast_to(line.astype(F32), (LANES, LANES)).T


def lane_bits(rows):
    return (iota((rows, LANES), 1) // TR) % FOLD


def spread_kernel(
    lanes_ref, code_ref, interp_hbm, near_ref, far_ref, base_ref, turn_ref, interp_ref, sem
):
    samples, _ = interp_ref.shape
    lon_tiles = NPHI // TPHI
    rows = min(512, samples)
    copies = []
    for step in range(samples // rows):
        here = pl.ds(step * rows, rows)
        copies.append(
            pltpu.make_async_copy(interp_hbm.at[here, :], interp_ref.at[here, :], sem.at[step])
        )
        copies[-1].start()

    place = iota((TPHI, 2 * LANES), 0)
    lane = iota((TPHI, 2 * LANES), 1)
    side = lane // LANES
    order = jnp.broadcast_to(lanes_ref[:1, :], (TPHI, 2 * LANES))
    turns = order * place + (NPHI // 4) * (side + lane % 2)
    angle = lax.bitwise_and(turns, NPHI - 1).astype(F32) * (2.0 * math.pi / NPHI)
    base = jnp.where(order == 0, 1.0, 2.0) * jnp.cos(angle)
    for i in range(TR):
        kept = jnp.where(lane % (LANES // 2) // (LANES // 2 // TR) == i, base, 0.0)
        base_ref[i * TPHI : (i + 1) * TPHI, :] = kept.astype(BF16)
    few = 2 * lon_tiles
    place, side, order = place[:few], side[:few], order[:few]
    turns = order * (place % lon_tiles) * TPHI + 3 * (NPHI // 4) * side
    angle = lax.bitwise_and(turns, NPHI - 1).astype(F32) * (2.0 * math.pi / NPHI)
    turn = jnp.cos(angle)
    rounded = turn.astype(BF16).astype(F32)
    turn = jnp.where(place < lon_tiles, rounded, turn - rounded)
    turn_ref[...] = jnp.zeros(turn_ref.shape, BF16)
    turn_ref[:few, :] = turn.astype(BF16)

    code = code_ref[...]
    lon_tile = lax.bitwise_and(code, lon_tiles - 1).astype(F32)
    cycle_tile = lax.shift_right_logical(code, lon_tiles.bit_length() - 1)
    low = lax.bitwise_and(cycle_tile, LOWS - 1).astype(F32).astype(BF16)
    high = lax.shift_right_logical(cycle_tile, LOWS.bit_length() - 1).astype(F32).astype(BF16)
    lines = samples // LANES
    for packet in (near_ref, far_ref):
        packet[samples // 2 : samples // 2 + lines, :] = low
        packet[samples // 2 + lines :, :] = high

    lane = iota((rows, LANES), 1)
    tile_of_lane = jnp.where(lane < few, lane % lon_tiles, -1).astype(F32)
    first = lane < LANES // 2
    before = []
    for step in range(samples // rows):
        groups = range(step * rows // LANES, (step + 1) * rows // LANES)
        columns = jnp.concatenate([column_of(lon_tile[g : g + 1, :]) for g in groups])
        tile_hit = jnp.where(columns == tile_of_lane, 1.0, 0.0).astype(BF16)
        turn = jnp.dot(tile_hit, turn_ref[...], preferred_element_type=F32)
        copies[step].wait()
        here = slice(step * rows, (step + 1) * rows)
        pair = jnp.dot(interp_ref[here, :], base_ref[...], preferred_element_type=F32) * turn
        both = pair[:, :LANES] + pair[:, LANES:]
        if step < samples // rows // 2:
            before.append(both)
            continue
        step -= samples // rows // 2
        here = slice(step * rows, (step + 1) * rows)
        swapped = pltpu.roll(both, LANES // 2, 1)
        near_ref[here, :] = jnp.where(first, before[step], swapped).astype(BF16)
        swapped = pltpu.roll(before[step], LANES // 2, 1)
        far_ref[here, :] = jnp.where(first, swapped, both).astype(BF16)


def spread_samples(order_lanes, code, interp):
    samples, pixels = interp.shape
    lines = samples // LANES
    packet = jax.ShapeDtypeStruct((samples // 2 + 2 * lines, LANES), BF16)
    return pl.pallas_call(
        spread_kernel,
        out_shape=(packet, packet),
        in_specs=[pl.BlockSpec(memory_space=pltpu.VMEM)] * 2
        + [pl.BlockSpec(memory_space=pltpu.HBM)],
        scratch_shapes=[
            pltpu.VMEM((pixels, 2 * LANES), BF16),
            pltpu.VMEM((LANES, 2 * LANES), BF16),
            pltpu.VMEM((samples, pixels), BF16),
            pltpu.SemaphoreType.DMA((samples // min(512, samples),)),
        ],
        compiler_params=pltpu.CompilerParams(vmem_limit_bytes=SMALL),
        name="spread_samples",
        cost_estimate=pl.CostEstimate(
            flops=samples * pixels * LANES * 16,
            bytes_accessed=samples * pixels * 4,
            transcendentals=0,
        ),
    )(order_lanes, code, in_hbm(interp))


def unpack_kernel(packet_ref, x_ref, low_ref, high_ref):
    samples = x_ref.shape[0]
    lines = samples // LANES
    rows = min(512, samples // 2)
    half = samples // 2
    for side in range(2):
        copy = copy_table(side * LANES // 2)
        for step in range(half // rows):
            part = packet_ref[step * rows : (step + 1) * rows, :]
            spread = jnp.dot(part, copy, preferred_element_type=F32)
            x_ref[side * half + step * rows : side * half + (step + 1) * rows, :] = spread.astype(BF16)
    low = packet_ref[half : half + lines, :].astype(F32)
    high = packet_ref[half + lines :, :].astype(F32)
    bits = lane_bits(LANES).astype(F32)
    for g in range(lines):
        here = slice(g * LANES, (g + 1) * LANES)
        low_ref[here, :] = (column_of(low[g : g + 1, :]) - bits).astype(BF16)
        high_ref[here, :] = column_of(high[g : g + 1, :]).astype(BF16)


def unpack_samples(packet, samples):
    return pl.pallas_call(
        unpack_kernel,
        out_shape=(
            jax.ShapeDtypeStruct((samples, FOLD * LANES // 2), BF16),
            jax.ShapeDtypeStruct((samples, LANES), BF16),
            jax.ShapeDtypeStruct((samples, LANES), BF16),
        ),
        in_specs=[pl.BlockSpec(memory_space=pltpu.VMEM)],
        compiler_params=pltpu.CompilerParams(vmem_limit_bytes=SMALL),
        name="unpack_samples",
        cost_estimate=pl.CostEstimate(
            flops=samples * LANES * LANES * 8, bytes_accessed=samples * LANES * 8, transcendentals=0
        ),
    )(packet)


def pick_kernel(counts, first_block, more, last, x_ref, low_ref, high_ref, *refs):
    stacks, rest = refs[: len(counts)], refs[len(counts) :]
    sums_ref = rest[0] if more else None
    out_ref, table_ref = rest[-2], rest[-1]
    samples = x_ref.shape[0]
    wide = table_ref.shape[1]
    steps, tile = LOWS // FOLD, FOLD * TR
    blocks = sum(counts) // (LANES // (2 * tile))
    j = 0
    for stack, count in zip(stacks, counts):
        for k in range(count):
            for c in range(2):
                for q in range(steps):
                    table_ref[pl.ds(q * blocks * LANES + (2 * j + c) * tile, tile), :] = stack[
                        pl.ds(k * LANES + (c * steps + q) * tile, tile), :
                    ]
            j += 1

    rows = min(512, samples)
    zero = jnp.zeros((rows, LANES), BF16)
    for step in range(samples // rows):
        here = slice(step * rows, (step + 1) * rows)
        low = low_ref[here, :]
        cut = [
            jnp.where(
                low == jnp.asarray(FOLD * q, BF16),
                x_ref[here, (first_block + b) * LANES : (first_block + b + 1) * LANES],
                zero,
            )
            for q in range(steps)
            for b in range(blocks)
        ]
        sums = jnp.dot(
            jnp.concatenate(cut, axis=1), table_ref[...], preferred_element_type=F32
        )
        if more:
            sums = sums + sums_ref[here, :]
        if not last:
            out_ref[here, :] = sums
            continue
        dets = out_ref.shape[0]
        sums = sums.astype(BF16)
        kept = []
        for b in range(wide // LANES):
            lane = ((iota((rows, LANES), 1) + LANES * b) // dets).astype(F32).astype(BF16)
            hit = high_ref[here, :] == lane
            kept.append(jnp.where(hit, sums[:, b * LANES : (b + 1) * LANES], zero))
        gather = iota((dets, wide), 1) % dets == iota((dets, wide), 0)
        gather = jnp.where(gather, 1.0, 0.0).astype(BF16)
        out_ref[:, here] = lax.dot_general(
            gather, jnp.concatenate(kept, axis=1), CONTRACT_LAST, preferred_element_type=F32
        ).astype(BF16)


def pick_values(x, low, high, stacks, first, sums, dets):
    samples = x.shape[0]
    counts = tuple(stack.shape[0] // LANES for stack in stacks)
    wide = stacks[0].shape[1]
    more = [] if sums is None else [sums]
    operands = [x, low, high, *stacks, *more]
    shape = ((samples, wide), F32) if dets is None else ((dets, samples), BF16)
    return pl.pallas_call(
        functools.partial(
            pick_kernel, counts, first * 2 * FOLD * TR // LANES, bool(more), dets is not None
        ),
        out_shape=jax.ShapeDtypeStruct(*shape),
        in_specs=[pl.BlockSpec(memory_space=pltpu.VMEM)] * len(operands),
        scratch_shapes=[pltpu.VMEM((sum(counts) * LANES, wide), BF16)],
        compiler_params=pltpu.CompilerParams(vmem_limit_bytes=16 * 2**20),
        name="pick_values",
        cost_estimate=pl.CostEstimate(
            flops=samples * sum(counts) * LANES * wide * 2, bytes_accessed=samples * 2048, transcendentals=0
        ),
    )(*operands)


def swap(value, axis, step):
    size = lax.axis_size(axis)
    return lax.ppermute(value, axis, [(i, i ^ step) for i in range(size)])


def in_chunks(piece, orders, code, interp, dets):
    chunks = orders.shape[0] // LOWS
    lanes = piece.shape[1]
    steps = LOWS // FOLD
    samples = interp.shape[0]
    gathered = lax.all_gather(piece, ("grp", "sub"), axis=0)
    gathered = gathered.reshape(chunks, LOWS, 2, steps, FOLD * TR, lanes)
    held = lane_order(iota((8, 2 * LANES), 1))

    def add_chunk(member, sums):
        packets = spread_samples(orders[member * LOWS + held], code, interp)
        near, far = [unpack_samples(packet, samples) for packet in packets]
        x, low = jnp.concatenate([near[0], far[0]], axis=1), near[1]
        table = lax.dynamic_index_in_dim(gathered, member, 0, False)
        table = table.transpose(2, 0, 1, 3, 4).reshape(steps, FOLD * LANES, lanes)
        for q in range(steps):
            hit = jnp.tile(low == FOLD * q, (1, FOLD))
            cut = jnp.where(hit, x, jnp.zeros_like(x))
            sums = sums + jnp.dot(cut, table[q], preferred_element_type=F32)
        return sums

    sums = lax.fori_loop(0, chunks, add_chunk, jnp.zeros((samples, lanes), F32))
    mark = code.reshape(-1) // ((NPHI // TPHI) * LOWS)
    hit = mark[:, None] == lax.iota(jnp.int32, lanes // dets)[None, :]
    sums = sums.reshape(samples, lanes // dets, dets)
    return jnp.sum(jnp.where(hit[:, :, None], sums, 0.0), axis=1).astype(BF16)


def on_device(alm, band_index, band_weight, legendre, orders, owner, tile_local, interp):
    group_count = lax.axis_size("grp")
    sub_count = lax.axis_size("sub")
    local_freqs = alm.shape[0]
    multipoles = alm.shape[3]
    cycles = legendre.shape[2]
    dets = band_weight.shape[0] // lax.axis_size("freq")
    samples = interp.shape[0]
    tiles_each = (cycles // (group_count * sub_count) // TR) * (NPHI // TPHI)
    far = sub_count // 2

    def slots(mine):
        return [
            (mine // sub_count ^ g) * sub_count + (mine % sub_count ^ s)
            for s in range(sub_count)
            for g in range(group_count)
        ][:LOWS]

    own, send, order_lanes, code = band_sums(
        band_index,
        band_weight,
        orders,
        owner[:, 0],
        tile_local,
        alm.reshape(local_freqs, 2, multipoles),
        tiles_each,
        slots,
    )
    received = swap(send, "freq", 1)
    if orders.shape[0] != LOWS:
        piece = cycle_coefs(own, received, legendre[0])
        return in_chunks(piece, orders, code, interp, dets)

    near_packet, far_packet = spread_samples(order_lanes, code, interp)
    got = swap(far_packet, "sub", far)
    received, near_packet = lax.optimization_barrier((received, near_packet))
    piece = cycle_coefs(own, received, legendre[0])
    gathered = [swap(piece, "grp", g) for g in range(1, group_count)]
    near_packet, _ = lax.optimization_barrier((near_packet, piece))
    near_x = unpack_samples(near_packet, samples)
    far_x = unpack_samples(got, samples)
    gathered, near_x, far_x = lax.optimization_barrier((gathered, near_x, far_x))
    stack = jnp.concatenate([piece] + gathered)
    stacks = [stack] + [swap(stack, "sub", s) for s in range(1, far)]
    sums = pick_values(*far_x, stacks[:1], 0, None, None)
    far_values = pick_values(*far_x, stacks[1:], group_count, sums, dets)
    other = swap(far_values, "sub", far)
    values = pick_values(*near_x, stacks, 0, None, dets)
    return (values.astype(F32) + other.astype(F32)).astype(BF16).T


def solution(mesh):
    placed = (
        P("freq", ("grp", "sub"), None, None),
        P(),
        P(),
        P(("grp", "sub"), None, None),
        P(),
        P(("grp", "sub"), None),
        P(("grp", "sub")),
        P(("grp", "sub"), None),
    )

    return jax.shard_map(
        on_device, mesh=mesh, in_specs=placed, out_specs=P(("grp", "sub"), "freq"), check_vma=False
    )
```

```python
import functools
import math

import jax
import jax.numpy as jnp
from jax import lax
from jax.experimental import pallas as pl
from jax.experimental.pallas import tpu as pltpu
from jax.sharding import PartitionSpec as P


NPHI = 1024
TR = 4
TPHI = 128
LANES = 128
LOWS = LANES // (2 * TR)
FOLD = 4
SMALL = 12 * 2**20
F32 = jnp.float32
BF16 = jnp.bfloat16
CONTRACT_LAST = (((1,), (1,)), ((), ()))


def iota(shape, axis):
    return lax.broadcasted_iota(jnp.int32, shape, axis)


def in_hbm(value):
    return pltpu.with_memory_space_constraint(value, pltpu.HBM)


def band_kernel(
    tiles_each, slots,
    index_ref, weight_ref, orders_ref, owner_ref, tile_ref, alm_ref,
    own_ref, send_ref, lanes_ref, code_ref,
    index, weight, orders, owner, tile, alm, sem
):
    sources = (index_ref, weight_ref, orders_ref, alm_ref, owner_ref, tile_ref)
    copies = [
        pltpu.make_async_copy(source, target, sem.at[n])
        for n, (source, target) in enumerate(zip(sources, (index, weight, orders, alm, owner, tile)))
    ]
    for copy in copies:
        copy.start()
    freqs, _, multipoles = alm.shape
    rows = 2 * freqs
    dets, entries = index.shape
    half = dets // 2
    me = lax.axis_index("freq")
    slot = lax.axis_index("grp") * lax.axis_size("sub") + lax.axis_index("sub")
    column = iota((dets, rows), 1)
    wanted = me * freqs + lax.shift_right_logical(column, 1)
    band = jnp.zeros((dets, rows), F32)
    copies[0].wait()
    copies[1].wait()
    for k in range(entries):
        hit = index[:, k : k + 1] == wanted
        band = band + jnp.where(hit, weight[:, k : k + 1], 0.0)
    part = lax.bitwise_and(column[:half], 1)
    low, high = band[:half], band[half:]
    own = jnp.where(me == 0, low, high)
    other = jnp.where(me == 0, high, low)
    matrix = jnp.concatenate(
        [jnp.where(part == c, side, 0.0) for side in (own, other) for c in range(2)]
    ).astype(BF16)
    copies[2].wait()
    keep = iota((dets, multipoles), 1) >= orders[slot]
    lane = iota(lanes_ref.shape, 1)
    held = lane_order(lane)
    order = jnp.zeros(lanes_ref.shape, jnp.int32)
    for j, here in enumerate(slots(slot)):
        order = jnp.where(held == j, orders[here], order)
    lanes_ref[...] = order
    copies[4].wait()
    copies[5].wait()
    code_ref[...] = owner[...] * tiles_each + tile[...]
    copies[3].wait()
    table = alm[...].reshape(rows, multipoles)
    sums = jnp.dot(matrix, table, preferred_element_type=F32)
    own_ref[...] = jnp.where(keep, sums[:dets], 0.0)
    send_ref[...] = jnp.where(keep, sums[dets:], 0.0).astype(BF16)


def lane_order(lane):
    half = LANES // 2
    return lane % (half // TR) // 2 + LOWS // 2 * (lane % LANES // half)


def band_sums(band_index, band_weight, orders, owner, tile, alm, tiles_each, slots):
    multipoles = alm.shape[2]
    dets = band_index.shape[0]
    lines = (owner.shape[0] // LANES, LANES)
    operands = (band_index, band_weight, orders, owner.reshape(lines), tile.reshape(lines), alm)
    return pl.pallas_call(
        functools.partial(band_kernel, tiles_each, slots),
        out_shape=(
            jax.ShapeDtypeStruct((dets, multipoles), F32),
            jax.ShapeDtypeStruct((dets, multipoles), BF16),
            jax.ShapeDtypeStruct((8, 2 * LANES), jnp.int32),
            jax.ShapeDtypeStruct(lines, jnp.int32),
        ),
        in_specs=[pl.BlockSpec(memory_space=pltpu.HBM)] * len(operands),
        scratch_shapes=[
            pltpu.VMEM(band_index.shape, jnp.int32),
            pltpu.VMEM(band_weight.shape, F32),
            pltpu.SMEM(orders.shape, jnp.int32),
            pltpu.VMEM(lines, jnp.int32),
            pltpu.VMEM(lines, jnp.int32),
            pltpu.VMEM(alm.shape, BF16),
            pltpu.SemaphoreType.DMA((len(operands),)),
        ],
        compiler_params=pltpu.CompilerParams(vmem_limit_bytes=SMALL),
        name="band_sums",
    )(*[in_hbm(value) for value in operands])


def cycle_kernel(own_ref, recv_ref, legendre_ref, out_ref):
    rows = own_ref.shape[0]
    half = rows // 2
    cycles = legendre_ref.shape[1]
    coefs = (own_ref[...] + recv_ref[...].astype(F32)).astype(BF16)
    table = jnp.dot(coefs, legendre_ref[...], preferred_element_type=F32)
    first = iota((half, LANES), 1) < LANES // 2
    lines = []
    for tile in range(cycles // LANES):
        both = table[:, tile * LANES : (tile + 1) * LANES]
        turned = pltpu.roll(both, LANES // 2, 1)
        lines.append(jnp.where(first, both[:half], turned[half:]))
        lines.append(jnp.where(first, turned[:half], both[half:]))
    each = LANES // half
    for block in range(len(lines) // each):
        square = jnp.concatenate(lines[block * each : (block + 1) * each])
        out_ref[:, block * LANES : (block + 1) * LANES] = square.T.astype(BF16)


def cycle_coefs(own, received, legendre):
    rows, _ = own.shape
    cycles = legendre.shape[1]
    return pl.pallas_call(
        cycle_kernel,
        out_shape=jax.ShapeDtypeStruct((LANES, rows * cycles // LANES), BF16),
        in_specs=[pl.BlockSpec(memory_space=pltpu.VMEM)] * 3,
        compiler_params=pltpu.CompilerParams(vmem_limit_bytes=SMALL),
        name="cycle_coefs",
    )(own, received, legendre)


def copy_table(first_row):
    parts = LANES // 2 // TR
    row = iota((LANES, FOLD * LANES // 2), 0) - first_row
    lane = iota((LANES, FOLD * LANES // 2), 1)
    hit = (row >= 0) & (row < LANES // 2)
    hit = hit & (row // parts == lane % TR) & (row % parts == lane // (FOLD * TR))
    return jnp.where(hit, 1.0, 0.0).astype(BF16)


def column_of(line):
    return jnp.broadcast_to(line.astype(F32), (LANES, LANES)).T


def lane_bits(rows):
    return (iota((rows, LANES), 1) // TR) % FOLD


def spread_kernel(
    lanes_ref, code_ref, interp_hbm, near_ref, far_ref, base_ref, turn_ref, interp_ref, sem
):
    samples, _ = interp_ref.shape
    lon_tiles = NPHI // TPHI
    rows = min(512, samples)
    copies = []
    for step in range(samples // rows):
        here = pl.ds(step * rows, rows)
        copies.append(
            pltpu.make_async_copy(interp_hbm.at[here, :], interp_ref.at[here, :], sem.at[step])
        )
        copies[-1].start()

    place = iota((TPHI, 2 * LANES), 0)
    lane = iota((TPHI, 2 * LANES), 1)
    side = lane // LANES
    order = jnp.broadcast_to(lanes_ref[:1, :], (TPHI, 2 * LANES))
    turns = order * place + (NPHI // 4) * (side + lane % 2)
    angle = lax.bitwise_and(turns, NPHI - 1).astype(F32) * (2.0 * math.pi / NPHI)
    base = jnp.where(order == 0, 1.0, 2.0) * jnp.cos(angle)
    for i in range(TR):
        kept = jnp.where(lane % (LANES // 2) // (LANES // 2 // TR) == i, base, 0.0)
        base_ref[i * TPHI : (i + 1) * TPHI, :] = kept.astype(BF16)
    few = 2 * lon_tiles
    place, side, order = place[:few], side[:few], order[:few]
    turns = order * (place % lon_tiles) * TPHI + 3 * (NPHI // 4) * side
    angle = lax.bitwise_and(turns, NPHI - 1).astype(F32) * (2.0 * math.pi / NPHI)
    turn = jnp.cos(angle)
    rounded = turn.astype(BF16).astype(F32)
    turn = jnp.where(place < lon_tiles, rounded, turn - rounded)
    turn_ref[...] = jnp.zeros(turn_ref.shape, BF16)
    turn_ref[:few, :] = turn.astype(BF16)

    code = code_ref[...]
    lon_tile = lax.bitwise_and(code, lon_tiles - 1).astype(F32)
    cycle_tile = lax.shift_right_logical(code, lon_tiles.bit_length() - 1)
    low = lax.bitwise_and(cycle_tile, LOWS - 1).astype(F32).astype(BF16)
    high = lax.shift_right_logical(cycle_tile, LOWS.bit_length() - 1).astype(F32).astype(BF16)
    lines = samples // LANES
    for packet in (near_ref, far_ref):
        packet[samples // 2 : samples // 2 + lines, :] = low
        packet[samples // 2 + lines :, :] = high

    lane = iota((rows, LANES), 1)
    tile_of_lane = jnp.where(lane < few, lane % lon_tiles, -1).astype(F32)
    first = lane < LANES // 2
    before = []
    for step in range(samples // rows):
        groups = range(step * rows // LANES, (step + 1) * rows // LANES)
        columns = jnp.concatenate([column_of(lon_tile[g : g + 1, :]) for g in groups])
        tile_hit = jnp.where(columns == tile_of_lane, 1.0, 0.0).astype(BF16)
        turn = jnp.dot(tile_hit, turn_ref[...], preferred_element_type=F32)
        copies[step].wait()
        here = slice(step * rows, (step + 1) * rows)
        pair = jnp.dot(interp_ref[here, :], base_ref[...], preferred_element_type=F32) * turn
        both = pair[:, :LANES] + pair[:, LANES:]
        if step < samples // rows // 2:
            before.append(both)
            continue
        step -= samples // rows // 2
        here = slice(step * rows, (step + 1) * rows)
        swapped = pltpu.roll(both, LANES // 2, 1)
        near_ref[here, :] = jnp.where(first, before[step], swapped).astype(BF16)
        swapped = pltpu.roll(before[step], LANES // 2, 1)
        far_ref[here, :] = jnp.where(first, swapped, both).astype(BF16)


def spread_samples(order_lanes, code, interp):
    samples, pixels = interp.shape
    lines = samples // LANES
    packet = jax.ShapeDtypeStruct((samples // 2 + 2 * lines, LANES), BF16)
    return pl.pallas_call(
        spread_kernel,
        out_shape=(packet, packet),
        in_specs=[pl.BlockSpec(memory_space=pltpu.VMEM)] * 2
        + [pl.BlockSpec(memory_space=pltpu.HBM)],
        scratch_shapes=[
            pltpu.VMEM((pixels, 2 * LANES), BF16),
            pltpu.VMEM((LANES, 2 * LANES), BF16),
            pltpu.VMEM((samples, pixels), BF16),
            pltpu.SemaphoreType.DMA((samples // min(512, samples),)),
        ],
        compiler_params=pltpu.CompilerParams(vmem_limit_bytes=SMALL),
        name="spread_samples",
        cost_estimate=pl.CostEstimate(
            flops=samples * pixels * LANES * 16,
            bytes_accessed=samples * pixels * 4,
            transcendentals=0,
        ),
    )(order_lanes, code, in_hbm(interp))


def unpack_kernel(packet_ref, x_ref, low_ref, high_ref):
    samples = x_ref.shape[0]
    lines = samples // LANES
    rows = min(512, samples // 2)
    half = samples // 2
    for side in range(2):
        copy = copy_table(side * LANES // 2)
        for step in range(half // rows):
            part = packet_ref[step * rows : (step + 1) * rows, :]
            spread = jnp.dot(part, copy, preferred_element_type=F32)
            x_ref[side * half + step * rows : side * half + (step + 1) * rows, :] = spread.astype(BF16)
    low = packet_ref[half : half + lines, :].astype(F32)
    high = packet_ref[half + lines :, :].astype(F32)
    bits = lane_bits(LANES).astype(F32)
    for g in range(lines):
        here = slice(g * LANES, (g + 1) * LANES)
        low_ref[here, :] = (column_of(low[g : g + 1, :]) - bits).astype(BF16)
        high_ref[here, :] = column_of(high[g : g + 1, :]).astype(BF16)


def unpack_samples(packet, samples):
    return pl.pallas_call(
        unpack_kernel,
        out_shape=(
            jax.ShapeDtypeStruct((samples, FOLD * LANES // 2), BF16),
            jax.ShapeDtypeStruct((samples, LANES), BF16),
            jax.ShapeDtypeStruct((samples, LANES), BF16),
        ),
        in_specs=[pl.BlockSpec(memory_space=pltpu.VMEM)],
        compiler_params=pltpu.CompilerParams(vmem_limit_bytes=SMALL),
        name="unpack_samples",
        cost_estimate=pl.CostEstimate(
            flops=samples * LANES * LANES * 8, bytes_accessed=samples * LANES * 8, transcendentals=0
        ),
    )(packet)


def pick_kernel(counts, first_block, more, last, x_ref, low_ref, high_ref, *refs):
    stacks, rest = refs[: len(counts)], refs[len(counts) :]
    sums_ref = rest[0] if more else None
    out_ref, table_ref, held_ref = rest[-3:]
    samples = x_ref.shape[0]
    steps, tile = LOWS // FOLD, FOLD * TR
    blocks = sum(counts) // (LANES // (2 * tile))
    j = 0
    for stack, count in zip(stacks, counts):
        for k in range(count):
            for c in range(2):
                for q in range(steps):
                    table_ref[pl.ds(q * blocks * LANES + (2 * j + c) * tile, tile), :] = stack[
                        pl.ds(k * LANES + (c * steps + q) * tile, tile), :
                    ]
            j += 1

    rows = min(512, samples)
    zero = jnp.zeros((rows, LANES), BF16)
    for step in range(samples // rows):
        here = slice(step * rows, (step + 1) * rows)
        low = low_ref[here, :]
        cut = [
            jnp.where(
                low == jnp.asarray(FOLD * q, BF16),
                x_ref[here, (first_block + b) * LANES : (first_block + b + 1) * LANES],
                zero,
            )
            for q in range(steps)
            for b in range(blocks)
        ]
        sums = jnp.dot(
            jnp.concatenate(cut, axis=1), table_ref[...], preferred_element_type=F32
        )
        if more:
            sums = sums + sums_ref[here, :]
        if last:
            held_ref[here, :] = sums
        else:
            out_ref[here, :] = sums
    if last:
        finish(held_ref, high_ref, out_ref, ())


def finish(sums_ref, high_ref, out_ref, more):
    samples, wide = sums_ref.shape
    dets = out_ref.shape[0]
    rows = min(512, samples)
    gather = iota((dets, wide), 1) % dets == iota((dets, wide), 0)
    gather = jnp.where(gather, 1.0, 0.0).astype(BF16)
    lanes = [
        ((iota((rows, LANES), 1) + LANES * b) // dets).astype(F32).astype(BF16)
        for b in range(wide // LANES)
    ]
    for step in range(samples // rows):
        here = slice(step * rows, (step + 1) * rows)
        kept = []
        for b, lane in enumerate(lanes):
            part = sums_ref[here, b * LANES : (b + 1) * LANES].astype(BF16)
            kept.append(jnp.where(high_ref[here, :] == lane, part, jnp.zeros_like(part)))
        values = lax.dot_general(
            gather, jnp.concatenate(kept, axis=1), CONTRACT_LAST, preferred_element_type=F32
        )
        for other in more:
            values = values + other[:, here].astype(F32)
        out_ref[:, here] = values.astype(BF16)


def pick_values(x, low, high, stacks, first, sums, dets):
    samples = x.shape[0]
    counts = tuple(stack.shape[0] // LANES for stack in stacks)
    wide = stacks[0].shape[1]
    more = [] if sums is None else [sums]
    operands = [x, low, high, *stacks, *more]
    shape = ((samples, wide), F32) if dets is None else ((dets, samples), BF16)
    return pl.pallas_call(
        functools.partial(
            pick_kernel, counts, first * 2 * FOLD * TR // LANES, bool(more), dets is not None
        ),
        out_shape=jax.ShapeDtypeStruct(*shape),
        in_specs=[pl.BlockSpec(memory_space=pltpu.VMEM)] * len(operands),
        scratch_shapes=[
            pltpu.VMEM((sum(counts) * LANES, wide), BF16),
            pltpu.VMEM((8 if dets is None else samples, wide), F32),
        ],
        compiler_params=pltpu.CompilerParams(vmem_limit_bytes=16 * 2**20),
        name="pick_values",
        cost_estimate=pl.CostEstimate(
            flops=samples * sum(counts) * LANES * wide * 2, bytes_accessed=samples * 2048, transcendentals=0
        ),
    )(*operands)


def swap(value, axis, step):
    size = lax.axis_size(axis)
    return lax.ppermute(value, axis, [(i, i ^ step) for i in range(size)])


def in_chunks(piece, orders, code, interp, dets):
    chunks = orders.shape[0] // LOWS
    lanes = piece.shape[1]
    steps = LOWS // FOLD
    samples = interp.shape[0]
    gathered = lax.all_gather(piece, ("grp", "sub"), axis=0)
    gathered = gathered.reshape(chunks, LOWS, 2, steps, FOLD * TR, lanes)
    held = lane_order(iota((8, 2 * LANES), 1))

    def add_chunk(member, sums):
        packets = spread_samples(orders[member * LOWS + held], code, interp)
        near, far = [unpack_samples(packet, samples) for packet in packets]
        x, low = jnp.concatenate([near[0], far[0]], axis=1), near[1]
        table = lax.dynamic_index_in_dim(gathered, member, 0, False)
        table = table.transpose(2, 0, 1, 3, 4).reshape(steps, FOLD * LANES, lanes)
        for q in range(steps):
            hit = jnp.tile(low == FOLD * q, (1, FOLD))
            cut = jnp.where(hit, x, jnp.zeros_like(x))
            sums = sums + jnp.dot(cut, table[q], preferred_element_type=F32)
        return sums

    sums = lax.fori_loop(0, chunks, add_chunk, jnp.zeros((samples, lanes), F32))
    mark = code.reshape(-1) // ((NPHI // TPHI) * LOWS)
    hit = mark[:, None] == lax.iota(jnp.int32, lanes // dets)[None, :]
    sums = sums.reshape(samples, lanes // dets, dets)
    return jnp.sum(jnp.where(hit[:, :, None], sums, 0.0), axis=1).astype(BF16)


def on_device(alm, band_index, band_weight, legendre, orders, owner, tile_local, interp):
    group_count = lax.axis_size("grp")
    sub_count = lax.axis_size("sub")
    local_freqs = alm.shape[0]
    multipoles = alm.shape[3]
    cycles = legendre.shape[2]
    dets = band_weight.shape[0] // lax.axis_size("freq")
    samples = interp.shape[0]
    tiles_each = (cycles // (group_count * sub_count) // TR) * (NPHI // TPHI)
    far = sub_count // 2

    def slots(mine):
        return [
            (mine // sub_count ^ g) * sub_count + (mine % sub_count ^ s)
            for s in range(sub_count)
            for g in range(group_count)
        ][:LOWS]

    own, send, order_lanes, code = band_sums(
        band_index,
        band_weight,
        orders,
        owner[:, 0],
        tile_local,
        alm.reshape(local_freqs, 2, multipoles),
        tiles_each,
        slots,
    )
    received = swap(send, "freq", 1)
    if orders.shape[0] != LOWS:
        piece = cycle_coefs(own, received, legendre[0])
        return in_chunks(piece, orders, code, interp, dets)

    near_packet, far_packet = spread_samples(order_lanes, code, interp)
    got = swap(far_packet, "sub", far)
    received, near_packet = lax.optimization_barrier((received, near_packet))
    piece = cycle_coefs(own, received, legendre[0])
    gathered = [swap(piece, "grp", g) for g in range(1, group_count)]
    near_packet, _ = lax.optimization_barrier((near_packet, piece))
    near_x = unpack_samples(near_packet, samples)
    far_x = unpack_samples(got, samples)
    gathered, near_x, far_x = lax.optimization_barrier((gathered, near_x, far_x))
    stack = jnp.concatenate([piece] + gathered)
    stacks = [stack] + [swap(stack, "sub", s) for s in range(1, far)]
    sums = pick_values(*far_x, stacks[:1], 0, None, None)
    far_values = pick_values(*far_x, stacks[1:], group_count, sums, dets)
    other = swap(far_values, "sub", far)
    values = pick_values(*near_x, stacks, 0, None, dets)
    return (values.astype(F32) + other.astype(F32)).astype(BF16).T


def solution(mesh):
    placed = (
        P("freq", ("grp", "sub"), None, None),
        P(),
        P(),
        P(("grp", "sub"), None, None),
        P(),
        P(("grp", "sub"), None),
        P(("grp", "sub")),
        P(("grp", "sub"), None),
    )

    return jax.shard_map(
        on_device, mesh=mesh, in_specs=placed, out_specs=P(("grp", "sub"), "freq"), check_vma=False
    )
```

```python
import functools
import math

import jax
import jax.numpy as jnp
from jax import lax
from jax.experimental import pallas as pl
from jax.experimental.pallas import tpu as pltpu
from jax.sharding import PartitionSpec as P


NPHI = 1024
TR = 4
TPHI = 128
LANES = 128
LOWS = LANES // (2 * TR)
FOLD = 4
SMALL = 12 * 2**20
F32 = jnp.float32
BF16 = jnp.bfloat16
CONTRACT_LAST = (((1,), (1,)), ((), ()))


def iota(shape, axis):
    return lax.broadcasted_iota(jnp.int32, shape, axis)


def in_hbm(value):
    return pltpu.with_memory_space_constraint(value, pltpu.HBM)


def band_kernel(
    tiles_each, slots,
    index_ref, weight_ref, orders_ref, owner_ref, tile_ref, alm_ref,
    own_ref, send_ref, lanes_ref, code_ref,
    index, weight, orders, owner, tile, alm, sem
):
    sources = (index_ref, weight_ref, orders_ref, alm_ref, owner_ref, tile_ref)
    copies = [
        pltpu.make_async_copy(source, target, sem.at[n])
        for n, (source, target) in enumerate(zip(sources, (index, weight, orders, alm, owner, tile)))
    ]
    for copy in copies:
        copy.start()
    freqs, _, multipoles = alm.shape
    rows = 2 * freqs
    dets, entries = index.shape
    half = dets // 2
    me = lax.axis_index("freq")
    slot = lax.axis_index("grp") * lax.axis_size("sub") + lax.axis_index("sub")
    column = iota((dets, rows), 1)
    wanted = me * freqs + lax.shift_right_logical(column, 1)
    band = jnp.zeros((dets, rows), F32)
    copies[0].wait()
    copies[1].wait()
    for k in range(entries):
        hit = index[:, k : k + 1] == wanted
        band = band + jnp.where(hit, weight[:, k : k + 1], 0.0)
    part = lax.bitwise_and(column[:half], 1)
    low, high = band[:half], band[half:]
    own = jnp.where(me == 0, low, high)
    other = jnp.where(me == 0, high, low)
    matrix = jnp.concatenate(
        [jnp.where(part == c, side, 0.0) for side in (own, other) for c in range(2)]
    ).astype(BF16)
    copies[2].wait()
    keep = iota((dets, multipoles), 1) >= orders[slot]
    lane = iota(lanes_ref.shape, 1)
    held = lane_order(lane)
    order = jnp.zeros(lanes_ref.shape, jnp.int32)
    for j, here in enumerate(slots(slot)):
        order = jnp.where(held == j, orders[here], order)
    lanes_ref[...] = order
    copies[4].wait()
    copies[5].wait()
    code_ref[...] = owner[...] * tiles_each + tile[...]
    copies[3].wait()
    table = alm[...].reshape(rows, multipoles)
    sums = jnp.dot(matrix, table, preferred_element_type=F32)
    own_ref[...] = jnp.where(keep, sums[:dets], 0.0)
    send_ref[...] = jnp.where(keep, sums[dets:], 0.0).astype(BF16)


def lane_order(lane):
    half = LANES // 2
    return lane % (half // TR) // 2 + LOWS // 2 * (lane % LANES // half)


def band_sums(band_index, band_weight, orders, owner, tile, alm, tiles_each, slots):
    multipoles = alm.shape[2]
    dets = band_index.shape[0]
    lines = (owner.shape[0] // LANES, LANES)
    operands = (band_index, band_weight, orders, owner.reshape(lines), tile.reshape(lines), alm)
    return pl.pallas_call(
        functools.partial(band_kernel, tiles_each, slots),
        out_shape=(
            jax.ShapeDtypeStruct((dets, multipoles), F32),
            jax.ShapeDtypeStruct((dets, multipoles), BF16),
            jax.ShapeDtypeStruct((8, 2 * LANES), jnp.int32),
            jax.ShapeDtypeStruct(lines, jnp.int32),
        ),
        in_specs=[pl.BlockSpec(memory_space=pltpu.HBM)] * len(operands),
        scratch_shapes=[
            pltpu.VMEM(band_index.shape, jnp.int32),
            pltpu.VMEM(band_weight.shape, F32),
            pltpu.SMEM(orders.shape, jnp.int32),
            pltpu.VMEM(lines, jnp.int32),
            pltpu.VMEM(lines, jnp.int32),
            pltpu.VMEM(alm.shape, BF16),
            pltpu.SemaphoreType.DMA((len(operands),)),
        ],
        compiler_params=pltpu.CompilerParams(vmem_limit_bytes=SMALL),
        name="band_sums",
        cost_estimate=pl.CostEstimate(
            flops=2**31, bytes_accessed=2**23, transcendentals=0
        ),
    )(*[in_hbm(value) for value in operands])


def cycle_kernel(own_ref, recv_ref, legendre_ref, out_ref):
    rows = own_ref.shape[0]
    half = rows // 2
    cycles = legendre_ref.shape[1]
    coefs = (own_ref[...] + recv_ref[...].astype(F32)).astype(BF16)
    table = jnp.dot(coefs, legendre_ref[...], preferred_element_type=F32)
    first = iota((half, LANES), 1) < LANES // 2
    lines = []
    for tile in range(cycles // LANES):
        both = table[:, tile * LANES : (tile + 1) * LANES]
        turned = pltpu.roll(both, LANES // 2, 1)
        lines.append(jnp.where(first, both[:half], turned[half:]))
        lines.append(jnp.where(first, turned[:half], both[half:]))
    each = LANES // half
    for block in range(len(lines) // each):
        square = jnp.concatenate(lines[block * each : (block + 1) * each])
        out_ref[:, block * LANES : (block + 1) * LANES] = square.T.astype(BF16)


def cycle_coefs(own, received, legendre):
    rows, _ = own.shape
    cycles = legendre.shape[1]
    return pl.pallas_call(
        cycle_kernel,
        out_shape=jax.ShapeDtypeStruct((LANES, rows * cycles // LANES), BF16),
        in_specs=[pl.BlockSpec(memory_space=pltpu.VMEM)] * 3,
        compiler_params=pltpu.CompilerParams(vmem_limit_bytes=SMALL),
        name="cycle_coefs",
    )(own, received, legendre)


def copy_table(first_row):
    parts = LANES // 2 // TR
    row = iota((LANES, FOLD * LANES // 2), 0) - first_row
    lane = iota((LANES, FOLD * LANES // 2), 1)
    hit = (row >= 0) & (row < LANES // 2)
    hit = hit & (row // parts == lane % TR) & (row % parts == lane // (FOLD * TR))
    return jnp.where(hit, 1.0, 0.0).astype(BF16)


def column_of(line):
    return jnp.broadcast_to(line.astype(F32), (LANES, LANES)).T


def lane_bits(rows):
    return (iota((rows, LANES), 1) // TR) % FOLD


def spread_kernel(
    lanes_ref, code_ref, interp_ref, near_ref, far_ref, base_ref, turn_ref
):
    samples, _ = interp_ref.shape
    lon_tiles = NPHI // TPHI
    rows = min(512, samples)
    place = iota((TPHI, 2 * LANES), 0)
    lane = iota((TPHI, 2 * LANES), 1)
    side = lane // LANES
    order = jnp.broadcast_to(lanes_ref[:1, :], (TPHI, 2 * LANES))
    turns = order * place + (NPHI // 4) * (side + lane % 2)
    angle = lax.bitwise_and(turns, NPHI - 1).astype(F32) * (2.0 * math.pi / NPHI)
    base = jnp.where(order == 0, 1.0, 2.0) * jnp.cos(angle)
    for i in range(TR):
        kept = jnp.where(lane % (LANES // 2) // (LANES // 2 // TR) == i, base, 0.0)
        base_ref[i * TPHI : (i + 1) * TPHI, :] = kept.astype(BF16)
    few = 2 * lon_tiles
    place, side, order = place[:few], side[:few], order[:few]
    turns = order * (place % lon_tiles) * TPHI + 3 * (NPHI // 4) * side
    angle = lax.bitwise_and(turns, NPHI - 1).astype(F32) * (2.0 * math.pi / NPHI)
    turn = jnp.cos(angle)
    rounded = turn.astype(BF16).astype(F32)
    turn = jnp.where(place < lon_tiles, rounded, turn - rounded)
    turn_ref[...] = jnp.zeros(turn_ref.shape, BF16)
    turn_ref[:few, :] = turn.astype(BF16)

    code = code_ref[...]
    lon_tile = lax.bitwise_and(code, lon_tiles - 1).astype(F32)
    cycle_tile = lax.shift_right_logical(code, lon_tiles.bit_length() - 1)
    low = lax.bitwise_and(cycle_tile, LOWS - 1).astype(F32).astype(BF16)
    high = lax.shift_right_logical(cycle_tile, LOWS.bit_length() - 1).astype(F32).astype(BF16)
    lines = samples // LANES
    for packet in (near_ref, far_ref):
        packet[samples // 2 : samples // 2 + lines, :] = low
        packet[samples // 2 + lines :, :] = high

    lane = iota((rows, LANES), 1)
    tile_of_lane = jnp.where(lane < few, lane % lon_tiles, -1).astype(F32)
    first = lane < LANES // 2
    before = []
    for step in range(samples // rows):
        groups = range(step * rows // LANES, (step + 1) * rows // LANES)
        columns = jnp.concatenate([column_of(lon_tile[g : g + 1, :]) for g in groups])
        tile_hit = jnp.where(columns == tile_of_lane, 1.0, 0.0).astype(BF16)
        turn = jnp.dot(tile_hit, turn_ref[...], preferred_element_type=F32)
        here = slice(step * rows, (step + 1) * rows)
        pair = jnp.dot(interp_ref[here, :], base_ref[...], preferred_element_type=F32) * turn
        both = pair[:, :LANES] + pair[:, LANES:]
        if step < samples // rows // 2:
            before.append(both)
            continue
        step -= samples // rows // 2
        here = slice(step * rows, (step + 1) * rows)
        swapped = pltpu.roll(both, LANES // 2, 1)
        near_ref[here, :] = jnp.where(first, before[step], swapped).astype(BF16)
        swapped = pltpu.roll(before[step], LANES // 2, 1)
        far_ref[here, :] = jnp.where(first, swapped, both).astype(BF16)


def spread_samples(order_lanes, code, interp):
    samples, pixels = interp.shape
    lines = samples // LANES
    packet = jax.ShapeDtypeStruct((samples // 2 + 2 * lines, LANES), BF16)
    return pl.pallas_call(
        spread_kernel,
        out_shape=(packet, packet),
        in_specs=[pl.BlockSpec(memory_space=pltpu.VMEM)] * 2
        + [pl.BlockSpec(memory_space=pltpu.VMEM)],
        scratch_shapes=[
            pltpu.VMEM((pixels, 2 * LANES), BF16),
            pltpu.VMEM((LANES, 2 * LANES), BF16),
        ],
        compiler_params=pltpu.CompilerParams(vmem_limit_bytes=SMALL),
        name="spread_samples",
        cost_estimate=pl.CostEstimate(
            flops=samples * pixels * LANES * 16,
            bytes_accessed=samples * pixels * 4,
            transcendentals=0,
        ),
    )(order_lanes, code, interp)


def unpack_kernel(packet_ref, x_ref, low_ref, high_ref):
    samples = x_ref.shape[0]
    lines = samples // LANES
    rows = min(512, samples // 2)
    half = samples // 2
    for side in range(2):
        copy = copy_table(side * LANES // 2)
        for step in range(half // rows):
            part = packet_ref[step * rows : (step + 1) * rows, :]
            spread = jnp.dot(part, copy, preferred_element_type=F32)
            x_ref[side * half + step * rows : side * half + (step + 1) * rows, :] = spread.astype(BF16)
    low = packet_ref[half : half + lines, :].astype(F32)
    high = packet_ref[half + lines :, :].astype(F32)
    bits = lane_bits(LANES).astype(F32)
    for g in range(lines):
        here = slice(g * LANES, (g + 1) * LANES)
        low_ref[here, :] = (column_of(low[g : g + 1, :]) - bits).astype(BF16)
        high_ref[here, :] = column_of(high[g : g + 1, :]).astype(BF16)


def unpack_samples(packet, samples):
    return pl.pallas_call(
        unpack_kernel,
        out_shape=(
            jax.ShapeDtypeStruct((samples, FOLD * LANES // 2), BF16),
            jax.ShapeDtypeStruct((samples, LANES), BF16),
            jax.ShapeDtypeStruct((samples, LANES), BF16),
        ),
        in_specs=[pl.BlockSpec(memory_space=pltpu.VMEM)],
        compiler_params=pltpu.CompilerParams(vmem_limit_bytes=SMALL),
        name="unpack_samples",
        cost_estimate=pl.CostEstimate(
            flops=samples * LANES * LANES * 8, bytes_accessed=samples * LANES * 8, transcendentals=0
        ),
    )(packet)


def pick_kernel(counts, first_block, more, last, x_ref, low_ref, high_ref, *refs):
    stacks, rest = refs[: len(counts)], refs[len(counts) :]
    sums_ref = rest[0] if more else None
    out_ref, table_ref, held_ref = rest[-3:]
    samples = x_ref.shape[0]
    steps, tile = LOWS // FOLD, FOLD * TR
    blocks = sum(counts) // (LANES // (2 * tile))
    j = 0
    for stack, count in zip(stacks, counts):
        for k in range(count):
            for c in range(2):
                for q in range(steps):
                    table_ref[pl.ds(q * blocks * LANES + (2 * j + c) * tile, tile), :] = stack[
                        pl.ds(k * LANES + (c * steps + q) * tile, tile), :
                    ]
            j += 1

    rows = min(512, samples)
    zero = jnp.zeros((rows, LANES), BF16)
    for step in range(samples // rows):
        here = slice(step * rows, (step + 1) * rows)
        low = low_ref[here, :]
        cut = [
            jnp.where(
                low == jnp.asarray(FOLD * q, BF16),
                x_ref[here, (first_block + b) * LANES : (first_block + b + 1) * LANES],
                zero,
            )
            for q in range(steps)
            for b in range(blocks)
        ]
        sums = jnp.dot(
            jnp.concatenate(cut, axis=1), table_ref[...], preferred_element_type=F32
        )
        if more:
            sums = sums + sums_ref[here, :]
        if last:
            held_ref[here, :] = sums
        else:
            out_ref[here, :] = sums
    if last:
        finish(held_ref, high_ref, out_ref, ())


def finish(sums_ref, high_ref, out_ref, more):
    samples, wide = sums_ref.shape
    dets = out_ref.shape[0]
    rows = min(512, samples)
    gather = iota((dets, wide), 1) % dets == iota((dets, wide), 0)
    gather = jnp.where(gather, 1.0, 0.0).astype(BF16)
    lanes = [
        ((iota((rows, LANES), 1) + LANES * b) // dets).astype(F32).astype(BF16)
        for b in range(wide // LANES)
    ]
    for step in range(samples // rows):
        here = slice(step * rows, (step + 1) * rows)
        kept = []
        for b, lane in enumerate(lanes):
            part = sums_ref[here, b * LANES : (b + 1) * LANES].astype(BF16)
            kept.append(jnp.where(high_ref[here, :] == lane, part, jnp.zeros_like(part)))
        values = lax.dot_general(
            gather, jnp.concatenate(kept, axis=1), CONTRACT_LAST, preferred_element_type=F32
        )
        for other in more:
            values = values + other[:, here].astype(F32)
        out_ref[:, here] = values.astype(BF16)


def pick_values(x, low, high, stacks, first, sums, dets):
    samples = x.shape[0]
    counts = tuple(stack.shape[0] // LANES for stack in stacks)
    wide = stacks[0].shape[1]
    more = [] if sums is None else [sums]
    operands = [x, low, high, *stacks, *more]
    shape = ((samples, wide), F32) if dets is None else ((dets, samples), BF16)
    return pl.pallas_call(
        functools.partial(
            pick_kernel, counts, first * 2 * FOLD * TR // LANES, bool(more), dets is not None
        ),
        out_shape=jax.ShapeDtypeStruct(*shape),
        in_specs=[pl.BlockSpec(memory_space=pltpu.VMEM)] * len(operands),
        scratch_shapes=[
            pltpu.VMEM((sum(counts) * LANES, wide), BF16),
            pltpu.VMEM((8 if dets is None else samples, wide), F32),
        ],
        compiler_params=pltpu.CompilerParams(vmem_limit_bytes=16 * 2**20),
        name="pick_values",
        cost_estimate=pl.CostEstimate(
            flops=samples * sum(counts) * LANES * wide * 2, bytes_accessed=samples * 2048, transcendentals=0
        ),
    )(*operands)


def swap(value, axis, step):
    size = lax.axis_size(axis)
    return lax.ppermute(value, axis, [(i, i ^ step) for i in range(size)])


def in_chunks(piece, orders, code, interp, dets):
    chunks = orders.shape[0] // LOWS
    lanes = piece.shape[1]
    steps = LOWS // FOLD
    samples = interp.shape[0]
    gathered = lax.all_gather(piece, ("grp", "sub"), axis=0)
    gathered = gathered.reshape(chunks, LOWS, 2, steps, FOLD * TR, lanes)
    held = lane_order(iota((8, 2 * LANES), 1))

    def add_chunk(member, sums):
        packets = spread_samples(orders[member * LOWS + held], code, interp)
        near, far = [unpack_samples(packet, samples) for packet in packets]
        x, low = jnp.concatenate([near[0], far[0]], axis=1), near[1]
        table = lax.dynamic_index_in_dim(gathered, member, 0, False)
        table = table.transpose(2, 0, 1, 3, 4).reshape(steps, FOLD * LANES, lanes)
        for q in range(steps):
            hit = jnp.tile(low == FOLD * q, (1, FOLD))
            cut = jnp.where(hit, x, jnp.zeros_like(x))
            sums = sums + jnp.dot(cut, table[q], preferred_element_type=F32)
        return sums

    sums = lax.fori_loop(0, chunks, add_chunk, jnp.zeros((samples, lanes), F32))
    mark = code.reshape(-1) // ((NPHI // TPHI) * LOWS)
    hit = mark[:, None] == lax.iota(jnp.int32, lanes // dets)[None, :]
    sums = sums.reshape(samples, lanes // dets, dets)
    return jnp.sum(jnp.where(hit[:, :, None], sums, 0.0), axis=1).astype(BF16)


def on_device(alm, band_index, band_weight, legendre, orders, owner, tile_local, interp):
    group_count = lax.axis_size("grp")
    sub_count = lax.axis_size("sub")
    local_freqs = alm.shape[0]
    multipoles = alm.shape[3]
    cycles = legendre.shape[2]
    dets = band_weight.shape[0] // lax.axis_size("freq")
    samples = interp.shape[0]
    tiles_each = (cycles // (group_count * sub_count) // TR) * (NPHI // TPHI)
    far = sub_count // 2

    def slots(mine):
        return [
            (mine // sub_count ^ g) * sub_count + (mine % sub_count ^ s)
            for s in range(sub_count)
            for g in range(group_count)
        ][:LOWS]

    own, send, order_lanes, code = band_sums(
        band_index,
        band_weight,
        orders,
        owner[:, 0],
        tile_local,
        alm.reshape(local_freqs, 2, multipoles),
        tiles_each,
        slots,
    )
    received = swap(send, "freq", 1)
    if orders.shape[0] != LOWS:
        piece = cycle_coefs(own, received, legendre[0])
        return in_chunks(piece, orders, code, interp, dets)

    near_packet, far_packet = spread_samples(order_lanes, code, interp)
    got = swap(far_packet, "sub", far)
    received, near_packet = lax.optimization_barrier((received, near_packet))
    piece = cycle_coefs(own, received, legendre[0])
    gathered = [swap(piece, "grp", g) for g in range(1, group_count)]
    near_packet, _ = lax.optimization_barrier((near_packet, piece))
    near_x = unpack_samples(near_packet, samples)
    far_x = unpack_samples(got, samples)
    gathered, near_x, far_x = lax.optimization_barrier((gathered, near_x, far_x))
    stack = jnp.concatenate([piece] + gathered)
    stacks = [stack] + [swap(stack, "sub", s) for s in range(1, far)]
    sums = pick_values(*far_x, stacks[:1], 0, None, None)
    far_values = pick_values(*far_x, stacks[1:], group_count, sums, dets)
    other = swap(far_values, "sub", far)
    values = pick_values(*near_x, stacks, 0, None, dets)
    return (values.astype(F32) + other.astype(F32)).astype(BF16).T


def solution(mesh):
    placed = (
        P("freq", ("grp", "sub"), None, None),
        P(),
        P(),
        P(("grp", "sub"), None, None),
        P(),
        P(("grp", "sub"), None),
        P(("grp", "sub")),
        P(("grp", "sub"), None),
    )

    return jax.shard_map(
        on_device, mesh=mesh, in_specs=placed, out_specs=P(("grp", "sub"), "freq"), check_vma=False
    )
```

```python
import functools
import math

import jax
import jax.numpy as jnp
from jax import lax
from jax.experimental import pallas as pl
from jax.experimental.pallas import tpu as pltpu
from jax.sharding import PartitionSpec as P


NPHI = 1024
TR = 4
TPHI = 128
LANES = 128
LOWS = LANES // (2 * TR)
FOLD = 4
SMALL = 12 * 2**20
F32 = jnp.float32
BF16 = jnp.bfloat16
CONTRACT_LAST = (((1,), (1,)), ((), ()))


def iota(shape, axis):
    return lax.broadcasted_iota(jnp.int32, shape, axis)


def in_hbm(value):
    return pltpu.with_memory_space_constraint(value, pltpu.HBM)


def band_kernel(
    tiles_each, slots,
    index_ref, weight_ref, orders_ref, owner_ref, tile_ref, alm_ref,
    own_ref, send_ref, lanes_ref, code_ref,
    index, weight, orders, owner, tile, alm, sem
):
    sources = (index_ref, weight_ref, orders_ref, alm_ref, owner_ref, tile_ref)
    copies = [
        pltpu.make_async_copy(source, target, sem.at[n])
        for n, (source, target) in enumerate(zip(sources, (index, weight, orders, alm, owner, tile)))
    ]
    for copy in copies:
        copy.start()
    freqs, _, multipoles = alm.shape
    rows = 2 * freqs
    dets, entries = index.shape
    half = dets // 2
    me = lax.axis_index("freq")
    slot = lax.axis_index("grp") * lax.axis_size("sub") + lax.axis_index("sub")
    column = iota((dets, rows), 1)
    wanted = me * freqs + lax.shift_right_logical(column, 1)
    band = jnp.zeros((dets, rows), F32)
    copies[0].wait()
    copies[1].wait()
    for k in range(entries):
        hit = index[:, k : k + 1] == wanted
        band = band + jnp.where(hit, weight[:, k : k + 1], 0.0)
    part = lax.bitwise_and(column[:half], 1)
    low, high = band[:half], band[half:]
    own = jnp.where(me == 0, low, high)
    other = jnp.where(me == 0, high, low)
    matrix = jnp.concatenate(
        [jnp.where(part == c, side, 0.0) for side in (own, other) for c in range(2)]
    ).astype(BF16)
    copies[2].wait()
    keep = iota((dets, multipoles), 1) >= orders[slot]
    lane = iota(lanes_ref.shape, 1)
    held = lane_order(lane)
    order = jnp.zeros(lanes_ref.shape, jnp.int32)
    for j, here in enumerate(slots(slot)):
        order = jnp.where(held == j, orders[here], order)
    lanes_ref[...] = order
    copies[4].wait()
    copies[5].wait()
    code_ref[...] = owner[...] * tiles_each + tile[...]
    copies[3].wait()
    table = alm[...].reshape(rows, multipoles)
    sums = jnp.dot(matrix, table, preferred_element_type=F32)
    own_ref[...] = jnp.where(keep, sums[:dets], 0.0)
    send_ref[...] = jnp.where(keep, sums[dets:], 0.0).astype(BF16)


def lane_order(lane):
    half = LANES // 2
    return lane % (half // TR) // 2 + LOWS // 2 * (lane % LANES // half)


def band_sums(band_index, band_weight, orders, owner, tile, alm, tiles_each, slots):
    multipoles = alm.shape[2]
    dets = band_index.shape[0]
    lines = (owner.shape[0] // LANES, LANES)
    operands = (band_index, band_weight, orders, owner.reshape(lines), tile.reshape(lines), alm)
    return pl.pallas_call(
        functools.partial(band_kernel, tiles_each, slots),
        out_shape=(
            jax.ShapeDtypeStruct((dets, multipoles), F32),
            jax.ShapeDtypeStruct((dets, multipoles), BF16),
            jax.ShapeDtypeStruct((8, 2 * LANES), jnp.int32),
            jax.ShapeDtypeStruct(lines, jnp.int32),
        ),
        in_specs=[pl.BlockSpec(memory_space=pltpu.HBM)] * len(operands),
        scratch_shapes=[
            pltpu.VMEM(band_index.shape, jnp.int32),
            pltpu.VMEM(band_weight.shape, F32),
            pltpu.SMEM(orders.shape, jnp.int32),
            pltpu.VMEM(lines, jnp.int32),
            pltpu.VMEM(lines, jnp.int32),
            pltpu.VMEM(alm.shape, BF16),
            pltpu.SemaphoreType.DMA((len(operands),)),
        ],
        compiler_params=pltpu.CompilerParams(vmem_limit_bytes=SMALL),
        name="band_sums",
        cost_estimate=pl.CostEstimate(
            flops=2**31, bytes_accessed=2**23, transcendentals=0
        ),
    )(*[in_hbm(value) for value in operands])


def cycle_kernel(own_ref, recv_ref, legendre_ref, out_ref):
    rows = own_ref.shape[0]
    half = rows // 2
    cycles = legendre_ref.shape[1]
    coefs = (own_ref[...] + recv_ref[...].astype(F32)).astype(BF16)
    table = jnp.dot(coefs, legendre_ref[...], preferred_element_type=F32)
    first = iota((half, LANES), 1) < LANES // 2
    lines = []
    for tile in range(cycles // LANES):
        both = table[:, tile * LANES : (tile + 1) * LANES]
        turned = pltpu.roll(both, LANES // 2, 1)
        lines.append(jnp.where(first, both[:half], turned[half:]))
        lines.append(jnp.where(first, turned[:half], both[half:]))
    each = LANES // half
    for block in range(len(lines) // each):
        square = jnp.concatenate(lines[block * each : (block + 1) * each])
        out_ref[:, block * LANES : (block + 1) * LANES] = square.T.astype(BF16)


def cycle_coefs(own, received, legendre):
    rows, _ = own.shape
    cycles = legendre.shape[1]
    return pl.pallas_call(
        cycle_kernel,
        out_shape=jax.ShapeDtypeStruct((LANES, rows * cycles // LANES), BF16),
        in_specs=[pl.BlockSpec(memory_space=pltpu.VMEM)] * 3,
        compiler_params=pltpu.CompilerParams(vmem_limit_bytes=SMALL),
        name="cycle_coefs",
    )(own, received, legendre)


def copy_table(first_row):
    parts = LANES // 2 // TR
    row = iota((LANES, FOLD * LANES // 2), 0) - first_row
    lane = iota((LANES, FOLD * LANES // 2), 1)
    hit = (row >= 0) & (row < LANES // 2)
    hit = hit & (row // parts == lane % TR) & (row % parts == lane // (FOLD * TR))
    return jnp.where(hit, 1.0, 0.0).astype(BF16)


def column_of(line):
    return jnp.broadcast_to(line.astype(F32), (LANES, LANES)).T


def lane_bits(rows):
    return (iota((rows, LANES), 1) // TR) % FOLD


def spread_kernel(
    lanes_ref, code_ref, interp_ref, near_ref, far_ref, base_ref, turn_ref
):
    samples, _ = interp_ref.shape
    lon_tiles = NPHI // TPHI
    rows = min(512, samples)
    place = iota((TPHI, 2 * LANES), 0)
    lane = iota((TPHI, 2 * LANES), 1)
    side = lane // LANES
    order = jnp.broadcast_to(lanes_ref[:1, :], (TPHI, 2 * LANES))
    turns = order * place + (NPHI // 4) * (side + lane % 2)
    angle = lax.bitwise_and(turns, NPHI - 1).astype(F32) * (2.0 * math.pi / NPHI)
    base = jnp.where(order == 0, 1.0, 2.0) * jnp.cos(angle)
    for i in range(TR):
        kept = jnp.where(lane % (LANES // 2) // (LANES // 2 // TR) == i, base, 0.0)
        base_ref[i * TPHI : (i + 1) * TPHI, :] = kept.astype(BF16)
    few = 2 * lon_tiles
    place, side, order = place[:few], side[:few], order[:few]
    turns = order * (place % lon_tiles) * TPHI + 3 * (NPHI // 4) * side
    angle = lax.bitwise_and(turns, NPHI - 1).astype(F32) * (2.0 * math.pi / NPHI)
    turn = jnp.cos(angle)
    rounded = turn.astype(BF16).astype(F32)
    turn = jnp.where(place < lon_tiles, rounded, turn - rounded)
    turn_ref[...] = jnp.zeros(turn_ref.shape, BF16)
    turn_ref[:few, :] = turn.astype(BF16)

    code = code_ref[...]
    lon_tile = lax.bitwise_and(code, lon_tiles - 1).astype(F32)
    cycle_tile = lax.shift_right_logical(code, lon_tiles.bit_length() - 1)
    low = lax.bitwise_and(cycle_tile, LOWS - 1).astype(F32).astype(BF16)
    high = lax.shift_right_logical(cycle_tile, LOWS.bit_length() - 1).astype(F32).astype(BF16)
    lines = samples // LANES
    for packet in (near_ref, far_ref):
        packet[samples // 2 : samples // 2 + lines, :] = low
        packet[samples // 2 + lines :, :] = high

    lane = iota((rows, LANES), 1)
    tile_of_lane = jnp.where(lane < few, lane % lon_tiles, -1).astype(F32)
    first = lane < LANES // 2
    before = []
    for step in range(samples // rows):
        groups = range(step * rows // LANES, (step + 1) * rows // LANES)
        columns = jnp.concatenate([column_of(lon_tile[g : g + 1, :]) for g in groups])
        tile_hit = jnp.where(columns == tile_of_lane, 1.0, 0.0).astype(BF16)
        turn = jnp.dot(tile_hit, turn_ref[...], preferred_element_type=F32)
        here = slice(step * rows, (step + 1) * rows)
        pair = jnp.dot(interp_ref[here, :], base_ref[...], preferred_element_type=F32) * turn
        both = pair[:, :LANES] + pair[:, LANES:]
        if step < samples // rows // 2:
            before.append(both)
            continue
        step -= samples // rows // 2
        here = slice(step * rows, (step + 1) * rows)
        swapped = pltpu.roll(both, LANES // 2, 1)
        near_ref[here, :] = jnp.where(first, before[step], swapped).astype(BF16)
        swapped = pltpu.roll(before[step], LANES // 2, 1)
        far_ref[here, :] = jnp.where(first, swapped, both).astype(BF16)


def spread_samples(order_lanes, code, interp):
    samples, pixels = interp.shape
    lines = samples // LANES
    packet = jax.ShapeDtypeStruct((samples // 2 + 2 * lines, LANES), BF16)
    return pl.pallas_call(
        spread_kernel,
        out_shape=(packet, packet),
        in_specs=[pl.BlockSpec(memory_space=pltpu.VMEM)] * 2
        + [pl.BlockSpec(memory_space=pltpu.VMEM)],
        scratch_shapes=[
            pltpu.VMEM((pixels, 2 * LANES), BF16),
            pltpu.VMEM((LANES, 2 * LANES), BF16),
        ],
        compiler_params=pltpu.CompilerParams(vmem_limit_bytes=SMALL),
        name="spread_samples",
        cost_estimate=pl.CostEstimate(
            flops=samples * pixels * LANES * 16,
            bytes_accessed=samples * pixels * 4,
            transcendentals=0,
        ),
    )(order_lanes, code, interp)


def unpack_kernel(packet_ref, x_ref, low_ref, high_ref):
    samples = x_ref.shape[0]
    lines = samples // LANES
    rows = min(512, samples // 2)
    half = samples // 2
    for side in range(2):
        copy = copy_table(side * LANES // 2)
        for step in range(half // rows):
            part = packet_ref[step * rows : (step + 1) * rows, :]
            spread = jnp.dot(part, copy, preferred_element_type=F32)
            x_ref[side * half + step * rows : side * half + (step + 1) * rows, :] = spread.astype(BF16)
    low = packet_ref[half : half + lines, :].astype(F32)
    high = packet_ref[half + lines :, :].astype(F32)
    bits = lane_bits(LANES).astype(F32)
    for g in range(lines):
        here = slice(g * LANES, (g + 1) * LANES)
        low_ref[here, :] = (column_of(low[g : g + 1, :]) - bits).astype(BF16)
        high_ref[here, :] = column_of(high[g : g + 1, :]).astype(BF16)


def unpack_samples(packet, samples):
    return pl.pallas_call(
        unpack_kernel,
        out_shape=(
            jax.ShapeDtypeStruct((samples, FOLD * LANES // 2), BF16),
            jax.ShapeDtypeStruct((samples, LANES), BF16),
            jax.ShapeDtypeStruct((samples, LANES), BF16),
        ),
        in_specs=[pl.BlockSpec(memory_space=pltpu.VMEM)],
        compiler_params=pltpu.CompilerParams(vmem_limit_bytes=SMALL),
        name="unpack_samples",
        cost_estimate=pl.CostEstimate(
            flops=samples * LANES * LANES * 8, bytes_accessed=samples * LANES * 8, transcendentals=0
        ),
    )(packet)


def pick_kernel(counts, first_block, more, last, x_ref, low_ref, high_ref, *refs):
    stacks, rest = refs[: len(counts)], refs[len(counts) :]
    sums_ref = rest[0] if more else None
    out_ref, table_ref, held_ref = rest[-3:]
    samples = x_ref.shape[0]
    steps, tile = LOWS // FOLD, FOLD * TR
    blocks = sum(counts) // (LANES // (2 * tile))
    j = 0
    for stack, count in zip(stacks, counts):
        for k in range(count):
            for c in range(2):
                for q in range(steps):
                    table_ref[pl.ds(q * blocks * LANES + (2 * j + c) * tile, tile), :] = stack[
                        pl.ds(k * LANES + (c * steps + q) * tile, tile), :
                    ]
            j += 1

    rows = min(512, samples)
    zero = jnp.zeros((rows, LANES), BF16)
    for step in range(samples // rows):
        here = slice(step * rows, (step + 1) * rows)
        low = low_ref[here, :]
        cut = [
            jnp.where(
                low == jnp.asarray(FOLD * q, BF16),
                x_ref[here, (first_block + b) * LANES : (first_block + b + 1) * LANES],
                zero,
            )
            for q in range(steps)
            for b in range(blocks)
        ]
        sums = jnp.dot(
            jnp.concatenate(cut, axis=1), table_ref[...], preferred_element_type=F32
        )
        if more:
            sums = sums + sums_ref[here, :]
        if last:
            held_ref[here, :] = sums
        else:
            out_ref[here, :] = sums
    if last:
        finish(held_ref, high_ref, out_ref, ())


def finish(sums_ref, high_ref, out_ref, more):
    samples, wide = sums_ref.shape
    dets = out_ref.shape[0]
    rows = min(512, samples)
    gather = iota((dets, wide), 1) % dets == iota((dets, wide), 0)
    gather = jnp.where(gather, 1.0, 0.0).astype(BF16)
    lanes = [
        ((iota((rows, LANES), 1) + LANES * b) // dets).astype(F32).astype(BF16)
        for b in range(wide // LANES)
    ]
    for step in range(samples // rows):
        here = slice(step * rows, (step + 1) * rows)
        kept = []
        for b, lane in enumerate(lanes):
            part = sums_ref[here, b * LANES : (b + 1) * LANES].astype(BF16)
            kept.append(jnp.where(high_ref[here, :] == lane, part, jnp.zeros_like(part)))
        values = lax.dot_general(
            gather, jnp.concatenate(kept, axis=1), CONTRACT_LAST, preferred_element_type=F32
        )
        for other in more:
            values = values + other[:, here].astype(F32)
        out_ref[:, here] = values.astype(BF16)


def pick_values(x, low, high, stacks, first, sums, dets):
    samples = x.shape[0]
    counts = tuple(stack.shape[0] // LANES for stack in stacks)
    wide = stacks[0].shape[1]
    more = [] if sums is None else [sums]
    operands = [x, low, high, *stacks, *more]
    shape = ((samples, wide), F32) if dets is None else ((dets, samples), BF16)
    return pl.pallas_call(
        functools.partial(
            pick_kernel, counts, first * 2 * FOLD * TR // LANES, bool(more), dets is not None
        ),
        out_shape=jax.ShapeDtypeStruct(*shape),
        in_specs=[pl.BlockSpec(memory_space=pltpu.VMEM)] * len(operands),
        scratch_shapes=[
            pltpu.VMEM((sum(counts) * LANES, wide), BF16),
            pltpu.VMEM((8 if dets is None else samples, wide), F32),
        ],
        compiler_params=pltpu.CompilerParams(vmem_limit_bytes=16 * 2**20),
        name="pick_values",
        cost_estimate=pl.CostEstimate(
            flops=samples * sum(counts) * LANES * wide * 2, bytes_accessed=samples * 2048, transcendentals=0
        ),
    )(*operands)


def swap(value, axis, step):
    size = lax.axis_size(axis)
    return lax.ppermute(value, axis, [(i, i ^ step) for i in range(size)])


def in_chunks(piece, orders, code, interp, dets):
    chunks = orders.shape[0] // LOWS
    lanes = piece.shape[1]
    steps = LOWS // FOLD
    samples = interp.shape[0]
    gathered = lax.all_gather(piece, ("grp", "sub"), axis=0)
    gathered = gathered.reshape(chunks, LOWS, 2, steps, FOLD * TR, lanes)
    held = lane_order(iota((8, 2 * LANES), 1))

    def add_chunk(member, sums):
        packets = spread_samples(orders[member * LOWS + held], code, interp)
        near, far = [unpack_samples(packet, samples) for packet in packets]
        x, low = jnp.concatenate([near[0], far[0]], axis=1), near[1]
        table = lax.dynamic_index_in_dim(gathered, member, 0, False)
        table = table.transpose(2, 0, 1, 3, 4).reshape(steps, FOLD * LANES, lanes)
        for q in range(steps):
            hit = jnp.tile(low == FOLD * q, (1, FOLD))
            cut = jnp.where(hit, x, jnp.zeros_like(x))
            sums = sums + jnp.dot(cut, table[q], preferred_element_type=F32)
        return sums

    sums = lax.fori_loop(0, chunks, add_chunk, jnp.zeros((samples, lanes), F32))
    mark = code.reshape(-1) // ((NPHI // TPHI) * LOWS)
    hit = mark[:, None] == lax.iota(jnp.int32, lanes // dets)[None, :]
    sums = sums.reshape(samples, lanes // dets, dets)
    return jnp.sum(jnp.where(hit[:, :, None], sums, 0.0), axis=1).astype(BF16)


def on_device(alm, band_index, band_weight, legendre, orders, owner, tile_local, interp):
    group_count = lax.axis_size("grp")
    sub_count = lax.axis_size("sub")
    local_freqs = alm.shape[0]
    multipoles = alm.shape[3]
    cycles = legendre.shape[2]
    dets = band_weight.shape[0] // lax.axis_size("freq")
    samples = interp.shape[0]
    tiles_each = (cycles // (group_count * sub_count) // TR) * (NPHI // TPHI)
    far = sub_count // 2

    def slots(mine):
        return [
            (mine // sub_count ^ g) * sub_count + (mine % sub_count ^ s)
            for s in range(sub_count)
            for g in range(group_count)
        ][:LOWS]

    own, send, order_lanes, code = band_sums(
        band_index,
        band_weight,
        orders,
        owner[:, 0],
        tile_local,
        alm.reshape(local_freqs, 2, multipoles),
        tiles_each,
        slots,
    )
    received = swap(send, "freq", 1)
    if orders.shape[0] != LOWS:
        piece = cycle_coefs(own, received, legendre[0])
        return in_chunks(piece, orders, code, interp, dets)

    near_packet, far_packet = spread_samples(order_lanes, code, interp)
    got = swap(far_packet, "sub", far)
    received, near_packet = lax.optimization_barrier((received, near_packet))
    piece = cycle_coefs(own, received, legendre[0])
    gathered = []
    for g in range(1, group_count):
        gathered.append(swap(piece, "grp", g))
    near_packet, _ = lax.optimization_barrier((near_packet, piece))
    near_x = unpack_samples(near_packet, samples)
    far_x = unpack_samples(got, samples)
    gathered[1], near_x, far_x = lax.optimization_barrier(
        (gathered[1], near_x, far_x)
    )
    pieces = [piece] + gathered
    others = []
    for s in range(1, far):
        for held in pieces:
            others.append(swap(held, "sub", s))
    sums = pick_values(*far_x, pieces, 0, None, None)
    far_values = pick_values(*far_x, others, group_count, sums, dets)
    other = swap(far_values, "sub", far)
    values = pick_values(*near_x, pieces + others, 0, None, dets)
    return (values.astype(F32) + other.astype(F32)).astype(BF16).T


def solution(mesh):
    placed = (
        P("freq", ("grp", "sub"), None, None),
        P(),
        P(),
        P(("grp", "sub"), None, None),
        P(),
        P(("grp", "sub"), None),
        P(("grp", "sub")),
        P(("grp", "sub"), None),
    )

    return jax.shard_map(
        on_device, mesh=mesh, in_specs=placed, out_specs=P(("grp", "sub"), "freq"), check_vma=False
    )
```

```python
import functools
import math

import jax
import jax.numpy as jnp
from jax import lax
from jax.experimental import pallas as pl
from jax.experimental.pallas import tpu as pltpu
from jax.sharding import PartitionSpec as P


NPHI = 1024
TR = 4
TPHI = 128
LANES = 128
LOWS = LANES // (2 * TR)
FOLD = 4
SMALL = 12 * 2**20
F32 = jnp.float32
BF16 = jnp.bfloat16
CONTRACT_LAST = (((1,), (1,)), ((), ()))


def iota(shape, axis):
    return lax.broadcasted_iota(jnp.int32, shape, axis)


def in_hbm(value):
    return pltpu.with_memory_space_constraint(value, pltpu.HBM)


def band_kernel(
    tiles_each, slots,
    index_ref, weight_ref, orders_ref, owner_ref, tile_ref, alm_ref,
    own_ref, send_ref, lanes_ref, code_ref,
    index, weight, orders, owner, tile, alm, sem
):
    sources = (index_ref, weight_ref, orders_ref, alm_ref, owner_ref, tile_ref)
    copies = [
        pltpu.make_async_copy(source, target, sem.at[n])
        for n, (source, target) in enumerate(zip(sources, (index, weight, orders, alm, owner, tile)))
    ]
    for copy in copies:
        copy.start()
    freqs, _, multipoles = alm.shape
    rows = 2 * freqs
    dets, entries = index.shape
    half = dets // 2
    me = lax.axis_index("freq")
    slot = lax.axis_index("grp") * lax.axis_size("sub") + lax.axis_index("sub")
    column = iota((dets, rows), 1)
    wanted = me * freqs + lax.shift_right_logical(column, 1)
    band = jnp.zeros((dets, rows), F32)
    copies[0].wait()
    copies[1].wait()
    for k in range(entries):
        hit = index[:, k : k + 1] == wanted
        band = band + jnp.where(hit, weight[:, k : k + 1], 0.0)
    part = lax.bitwise_and(column[:half], 1)
    low, high = band[:half], band[half:]
    own = jnp.where(me == 0, low, high)
    other = jnp.where(me == 0, high, low)
    matrix = jnp.concatenate(
        [jnp.where(part == c, side, 0.0) for side in (own, other) for c in range(2)]
    ).astype(BF16)
    copies[2].wait()
    keep = iota((dets, multipoles), 1) >= orders[slot]
    lane = iota(lanes_ref.shape, 1)
    held = lane_order(lane)
    order = jnp.zeros(lanes_ref.shape, jnp.int32)
    for j, here in enumerate(slots(slot)):
        order = jnp.where(held == j, orders[here], order)
    lanes_ref[...] = order
    copies[4].wait()
    copies[5].wait()
    code_ref[...] = owner[...] * tiles_each + tile[...]
    copies[3].wait()
    table = alm[...].reshape(rows, multipoles)
    sums = jnp.dot(matrix, table, preferred_element_type=F32)
    own_ref[...] = jnp.where(keep, sums[:dets], 0.0)
    send_ref[...] = jnp.where(keep, sums[dets:], 0.0).astype(BF16)


def lane_order(lane):
    half = LANES // 2
    return lane % (half // TR) // 2 + LOWS // 2 * (lane % LANES // half)


def band_sums(band_index, band_weight, orders, owner, tile, alm, tiles_each, slots):
    multipoles = alm.shape[2]
    dets = band_index.shape[0]
    lines = (owner.shape[0] // LANES, LANES)
    operands = (band_index, band_weight, orders, owner.reshape(lines), tile.reshape(lines), alm)
    return pl.pallas_call(
        functools.partial(band_kernel, tiles_each, slots),
        out_shape=(
            jax.ShapeDtypeStruct((dets, multipoles), F32),
            jax.ShapeDtypeStruct((dets, multipoles), BF16),
            jax.ShapeDtypeStruct((8, 2 * LANES), jnp.int32),
            jax.ShapeDtypeStruct(lines, jnp.int32),
        ),
        in_specs=[pl.BlockSpec(memory_space=pltpu.HBM)] * len(operands),
        scratch_shapes=[
            pltpu.VMEM(band_index.shape, jnp.int32),
            pltpu.VMEM(band_weight.shape, F32),
            pltpu.SMEM(orders.shape, jnp.int32),
            pltpu.VMEM(lines, jnp.int32),
            pltpu.VMEM(lines, jnp.int32),
            pltpu.VMEM(alm.shape, BF16),
            pltpu.SemaphoreType.DMA((len(operands),)),
        ],
        compiler_params=pltpu.CompilerParams(vmem_limit_bytes=SMALL),
        name="band_sums",
        cost_estimate=pl.CostEstimate(
            flops=2**31, bytes_accessed=2**23, transcendentals=0
        ),
    )(*[in_hbm(value) for value in operands])


def cycle_kernel(own_ref, recv_ref, legendre_ref, out_ref):
    rows = own_ref.shape[0]
    half = rows // 2
    cycles = legendre_ref.shape[1]
    coefs = (own_ref[...] + recv_ref[...].astype(F32)).astype(BF16)
    table = jnp.dot(coefs, legendre_ref[...], preferred_element_type=F32)
    first = iota((half, LANES), 1) < LANES // 2
    lines = []
    for tile in range(cycles // LANES):
        both = table[:, tile * LANES : (tile + 1) * LANES]
        turned = pltpu.roll(both, LANES // 2, 1)
        lines.append(jnp.where(first, both[:half], turned[half:]))
        lines.append(jnp.where(first, turned[:half], both[half:]))
    each = LANES // half
    for block in range(len(lines) // each):
        square = jnp.concatenate(lines[block * each : (block + 1) * each])
        out_ref[:, block * LANES : (block + 1) * LANES] = square.T.astype(BF16)


def cycle_coefs(own, received, legendre):
    rows, _ = own.shape
    cycles = legendre.shape[1]
    return pl.pallas_call(
        cycle_kernel,
        out_shape=jax.ShapeDtypeStruct((LANES, rows * cycles // LANES), BF16),
        in_specs=[pl.BlockSpec(memory_space=pltpu.VMEM)] * 3,
        compiler_params=pltpu.CompilerParams(vmem_limit_bytes=SMALL),
        name="cycle_coefs",
    )(own, received, legendre)


def copy_table(first_row):
    parts = LANES // 2 // TR
    row = iota((LANES, FOLD * LANES // 2), 0) - first_row
    lane = iota((LANES, FOLD * LANES // 2), 1)
    hit = (row >= 0) & (row < LANES // 2)
    hit = hit & (row // parts == lane % TR) & (row % parts == lane // (FOLD * TR))
    return jnp.where(hit, 1.0, 0.0).astype(BF16)


def column_of(line):
    return jnp.broadcast_to(line.astype(F32), (LANES, LANES)).T


def lane_bits(rows):
    return (iota((rows, LANES), 1) // TR) % FOLD


def spread_kernel(
    lanes_ref, code_ref, interp_ref, near_ref, far_ref, base_ref, turn_ref
):
    samples, _ = interp_ref.shape
    lon_tiles = NPHI // TPHI
    rows = min(512, samples)
    place = iota((TPHI, 2 * LANES), 0)
    lane = iota((TPHI, 2 * LANES), 1)
    side = lane // LANES
    order = jnp.broadcast_to(lanes_ref[:1, :], (TPHI, 2 * LANES))
    turns = order * place + (NPHI // 4) * (side + lane % 2)
    angle = lax.bitwise_and(turns, NPHI - 1).astype(F32) * (2.0 * math.pi / NPHI)
    base = jnp.where(order == 0, 1.0, 2.0) * jnp.cos(angle)
    for i in range(TR):
        kept = jnp.where(lane % (LANES // 2) // (LANES // 2 // TR) == i, base, 0.0)
        base_ref[i * TPHI : (i + 1) * TPHI, :] = kept.astype(BF16)
    few = 2 * lon_tiles
    place, side, order = place[:few], side[:few], order[:few]
    turns = order * (place % lon_tiles) * TPHI + 3 * (NPHI // 4) * side
    angle = lax.bitwise_and(turns, NPHI - 1).astype(F32) * (2.0 * math.pi / NPHI)
    turn = jnp.cos(angle)
    rounded = turn.astype(BF16).astype(F32)
    turn = jnp.where(place < lon_tiles, rounded, turn - rounded)
    turn_ref[...] = jnp.zeros(turn_ref.shape, BF16)
    turn_ref[:few, :] = turn.astype(BF16)

    code = code_ref[...]
    lon_tile = lax.bitwise_and(code, lon_tiles - 1).astype(F32)
    cycle_tile = lax.shift_right_logical(code, lon_tiles.bit_length() - 1)
    low = lax.bitwise_and(cycle_tile, LOWS - 1).astype(F32).astype(BF16)
    high = lax.shift_right_logical(cycle_tile, LOWS.bit_length() - 1).astype(F32).astype(BF16)
    lines = samples // LANES
    for packet in (near_ref, far_ref):
        packet[samples // 2 : samples // 2 + lines, :] = low
        packet[samples // 2 + lines :, :] = high

    lane = iota((rows, LANES), 1)
    tile_of_lane = jnp.where(lane < few, lane % lon_tiles, -1).astype(F32)
    first = lane < LANES // 2
    before = []
    for step in range(samples // rows):
        groups = range(step * rows // LANES, (step + 1) * rows // LANES)
        columns = jnp.concatenate([column_of(lon_tile[g : g + 1, :]) for g in groups])
        tile_hit = jnp.where(columns == tile_of_lane, 1.0, 0.0).astype(BF16)
        turn = jnp.dot(tile_hit, turn_ref[...], preferred_element_type=F32)
        here = slice(step * rows, (step + 1) * rows)
        pair = jnp.dot(interp_ref[here, :], base_ref[...], preferred_element_type=F32) * turn
        both = pair[:, :LANES] + pair[:, LANES:]
        if step < samples // rows // 2:
            before.append(both)
            continue
        step -= samples // rows // 2
        here = slice(step * rows, (step + 1) * rows)
        swapped = pltpu.roll(both, LANES // 2, 1)
        near_ref[here, :] = jnp.where(first, before[step], swapped).astype(BF16)
        swapped = pltpu.roll(before[step], LANES // 2, 1)
        far_ref[here, :] = jnp.where(first, swapped, both).astype(BF16)


def spread_samples(order_lanes, code, interp):
    samples, pixels = interp.shape
    lines = samples // LANES
    packet = jax.ShapeDtypeStruct((samples // 2 + 2 * lines, LANES), BF16)
    return pl.pallas_call(
        spread_kernel,
        out_shape=(packet, packet),
        in_specs=[pl.BlockSpec(memory_space=pltpu.VMEM)] * 2
        + [pl.BlockSpec(memory_space=pltpu.VMEM)],
        scratch_shapes=[
            pltpu.VMEM((pixels, 2 * LANES), BF16),
            pltpu.VMEM((LANES, 2 * LANES), BF16),
        ],
        compiler_params=pltpu.CompilerParams(vmem_limit_bytes=SMALL),
        name="spread_samples",
        cost_estimate=pl.CostEstimate(
            flops=samples * pixels * LANES * 16,
            bytes_accessed=samples * pixels * 4,
            transcendentals=0,
        ),
    )(order_lanes, code, interp)


def unpack_kernel(packet_ref, x_ref, low_ref, high_ref):
    samples = x_ref.shape[0]
    lines = samples // LANES
    rows = min(512, samples // 2)
    half = samples // 2
    for side in range(2):
        copy = copy_table(side * LANES // 2)
        for step in range(half // rows):
            part = packet_ref[step * rows : (step + 1) * rows, :]
            spread = jnp.dot(part, copy, preferred_element_type=F32)
            x_ref[side * half + step * rows : side * half + (step + 1) * rows, :] = spread.astype(BF16)
    low = packet_ref[half : half + lines, :].astype(F32)
    high = packet_ref[half + lines :, :].astype(F32)
    bits = lane_bits(LANES).astype(F32)
    for g in range(lines):
        here = slice(g * LANES, (g + 1) * LANES)
        low_ref[here, :] = (column_of(low[g : g + 1, :]) - bits).astype(BF16)
        high_ref[here, :] = column_of(high[g : g + 1, :]).astype(BF16)


def unpack_samples(packet, samples):
    return pl.pallas_call(
        unpack_kernel,
        out_shape=(
            jax.ShapeDtypeStruct((samples, FOLD * LANES // 2), BF16),
            jax.ShapeDtypeStruct((samples, LANES), BF16),
            jax.ShapeDtypeStruct((samples, LANES), BF16),
        ),
        in_specs=[pl.BlockSpec(memory_space=pltpu.VMEM)],
        compiler_params=pltpu.CompilerParams(vmem_limit_bytes=SMALL),
        name="unpack_samples",
        cost_estimate=pl.CostEstimate(
            flops=samples * LANES * LANES * 8, bytes_accessed=samples * LANES * 8, transcendentals=0
        ),
    )(packet)


def pick_kernel(counts, first_block, more, last, x_ref, low_ref, high_ref, *refs):
    stacks, rest = refs[: len(counts)], refs[len(counts) :]
    sums_ref = rest[0] if more else None
    out_ref, table_ref, held_ref = rest[-3:]
    samples = x_ref.shape[0]
    steps, tile = LOWS // FOLD, FOLD * TR
    blocks = sum(counts) // (LANES // (2 * tile))
    j = 0
    for stack, count in zip(stacks, counts):
        for k in range(count):
            for c in range(2):
                for q in range(steps):
                    table_ref[pl.ds(q * blocks * LANES + (2 * j + c) * tile, tile), :] = stack[
                        pl.ds(k * LANES + (c * steps + q) * tile, tile), :
                    ]
            j += 1

    rows = min(512, samples)
    zero = jnp.zeros((rows, LANES), BF16)
    for step in range(samples // rows):
        here = slice(step * rows, (step + 1) * rows)
        low = low_ref[here, :]
        cut = [
            jnp.where(
                low == jnp.asarray(FOLD * q, BF16),
                x_ref[here, (first_block + b) * LANES : (first_block + b + 1) * LANES],
                zero,
            )
            for q in range(steps)
            for b in range(blocks)
        ]
        sums = jnp.dot(
            jnp.concatenate(cut, axis=1), table_ref[...], preferred_element_type=F32
        )
        if more:
            sums = sums + sums_ref[here, :]
        if last:
            held_ref[here, :] = sums.astype(BF16)
        else:
            out_ref[here, :] = sums
    if last:
        finish(held_ref, high_ref, out_ref)


def finish(sums_ref, high_ref, out_ref):
    samples, wide = sums_ref.shape
    dets = out_ref.shape[0]
    rows = min(512, samples)
    gather = iota((dets, wide), 1) % dets == iota((dets, wide), 0)
    gather = jnp.where(gather, 1.0, 0.0).astype(BF16)
    lanes = [
        ((iota((rows, LANES), 1) + LANES * b) // dets).astype(F32).astype(BF16)
        for b in range(wide // LANES)
    ]
    for step in range(samples // rows):
        here = slice(step * rows, (step + 1) * rows)
        kept = []
        for b, lane in enumerate(lanes):
            part = sums_ref[here, b * LANES : (b + 1) * LANES]
            kept.append(jnp.where(high_ref[here, :] == lane, part, jnp.zeros_like(part)))
        values = lax.dot_general(
            gather, jnp.concatenate(kept, axis=1), CONTRACT_LAST, preferred_element_type=F32
        )
        out_ref[:, here] = values.astype(BF16)


def pick_values(x, low, high, stacks, first, sums, dets):
    samples = x.shape[0]
    counts = tuple(stack.shape[0] // LANES for stack in stacks)
    wide = stacks[0].shape[1]
    more = [] if sums is None else [sums]
    operands = [x, low, high, *stacks, *more]
    shape = ((samples, wide), F32) if dets is None else ((dets, samples), BF16)
    return pl.pallas_call(
        functools.partial(
            pick_kernel, counts, first * 2 * FOLD * TR // LANES, bool(more), dets is not None
        ),
        out_shape=jax.ShapeDtypeStruct(*shape),
        in_specs=[pl.BlockSpec(memory_space=pltpu.VMEM)] * len(operands),
        scratch_shapes=[
            pltpu.VMEM((sum(counts) * LANES, wide), BF16),
            pltpu.VMEM((16 if dets is None else samples, wide), BF16),
        ],
        compiler_params=pltpu.CompilerParams(vmem_limit_bytes=16 * 2**20),
        name="pick_values",
        cost_estimate=pl.CostEstimate(
            flops=samples * sum(counts) * LANES * wide * 2, bytes_accessed=samples * 2048, transcendentals=0
        ),
    )(*operands)


def swap(value, axis, step):
    size = lax.axis_size(axis)
    return lax.ppermute(value, axis, [(i, i ^ step) for i in range(size)])


def in_chunks(piece, orders, code, interp, dets):
    chunks = orders.shape[0] // LOWS
    lanes = piece.shape[1]
    steps = LOWS // FOLD
    samples = interp.shape[0]
    gathered = lax.all_gather(piece, ("grp", "sub"), axis=0)
    gathered = gathered.reshape(chunks, LOWS, 2, steps, FOLD * TR, lanes)
    held = lane_order(iota((8, 2 * LANES), 1))

    def add_chunk(member, sums):
        packets = spread_samples(orders[member * LOWS + held], code, interp)
        near, far = [unpack_samples(packet, samples) for packet in packets]
        x, low = jnp.concatenate([near[0], far[0]], axis=1), near[1]
        table = lax.dynamic_index_in_dim(gathered, member, 0, False)
        table = table.transpose(2, 0, 1, 3, 4).reshape(steps, FOLD * LANES, lanes)
        for q in range(steps):
            hit = jnp.tile(low == FOLD * q, (1, FOLD))
            cut = jnp.where(hit, x, jnp.zeros_like(x))
            sums = sums + jnp.dot(cut, table[q], preferred_element_type=F32)
        return sums

    sums = lax.fori_loop(0, chunks, add_chunk, jnp.zeros((samples, lanes), F32))
    mark = code.reshape(-1) // ((NPHI // TPHI) * LOWS)
    hit = mark[:, None] == lax.iota(jnp.int32, lanes // dets)[None, :]
    sums = sums.reshape(samples, lanes // dets, dets)
    return jnp.sum(jnp.where(hit[:, :, None], sums, 0.0), axis=1).astype(BF16)


def on_device(alm, band_index, band_weight, legendre, orders, owner, tile_local, interp):
    group_count = lax.axis_size("grp")
    sub_count = lax.axis_size("sub")
    local_freqs = alm.shape[0]
    multipoles = alm.shape[3]
    cycles = legendre.shape[2]
    dets = band_weight.shape[0] // lax.axis_size("freq")
    samples = interp.shape[0]
    tiles_each = (cycles // (group_count * sub_count) // TR) * (NPHI // TPHI)
    far = sub_count // 2

    def slots(mine):
        return [
            (mine // sub_count ^ g) * sub_count + (mine % sub_count ^ s)
            for s in range(sub_count)
            for g in range(group_count)
        ][:LOWS]

    own, send, order_lanes, code = band_sums(
        band_index,
        band_weight,
        orders,
        owner[:, 0],
        tile_local,
        alm.reshape(local_freqs, 2, multipoles),
        tiles_each,
        slots,
    )
    received = swap(send, "freq", 1)
    if orders.shape[0] != LOWS:
        piece = cycle_coefs(own, received, legendre[0])
        return in_chunks(piece, orders, code, interp, dets)

    near_packet, far_packet = spread_samples(order_lanes, code, interp)
    got = swap(far_packet, "sub", far)
    received, near_packet = lax.optimization_barrier((received, near_packet))
    piece = cycle_coefs(own, received, legendre[0])
    gathered = []
    for g in range(1, group_count):
        gathered.append(swap(piece, "grp", g))
    near_packet, _ = lax.optimization_barrier((near_packet, piece))
    near_x = unpack_samples(near_packet, samples)
    far_x = unpack_samples(got, samples)
    gathered[1:], near_x, far_x = lax.optimization_barrier((gathered[1:], near_x, far_x))
    pieces = [piece] + gathered
    others = []
    for s in range(1, far):
        for held in pieces:
            others.append(swap(held, "sub", s))
    sums = pick_values(*far_x, pieces, 0, None, None)
    far_values = pick_values(*far_x, others, group_count, sums, dets)
    other = swap(far_values, "sub", far)
    values = pick_values(*near_x, pieces + others, 0, None, dets)
    return (values.astype(F32) + other.astype(F32)).astype(BF16).T


def solution(mesh):
    placed = (
        P("freq", ("grp", "sub"), None, None),
        P(),
        P(),
        P(("grp", "sub"), None, None),
        P(),
        P(("grp", "sub"), None),
        P(("grp", "sub")),
        P(("grp", "sub"), None),
    )

    return jax.shard_map(
        on_device, mesh=mesh, in_specs=placed, out_specs=P(("grp", "sub"), "freq"), check_vma=False
    )
```
